512 devices in a mesh: cons: 4 (over y_hi), ty: 8 (over x, y_lo), tx: 16 (over z, core).
Axes of the slice: x: 4, y: 8 (y_hi: 4, y_lo: 2; y = y_hi * 2 + y_lo), z: 8, core: 2. Of those that a mesh axis runs over, the one named last changes fastest.
Arguments:
- elevation: float32 [8, 2, 1152, 8192], P('cons', None, 'ty', 'tx'), may hold values from -6 to 6
- equilibrium: float32 [8, 2, 1152, 8192], P('cons', None, 'ty', 'tx'), may hold values from -5 to 5
- depth: float32 [1152, 8192], P('ty', 'tx'), may hold values from 0.1 to 1
- land_mask: int32 [1152, 8192], P('ty', 'tx'), may hold values 0 or 1
- friction_prev: float32 [1152, 8192], P('ty', 'tx'), may hold values from 0.3 to 3
Outputs:
- elevation_out: float32 [8, 2, 1152, 8192], P('cons', None, 'ty', 'tx')
- friction: float32 [1152, 8192], P('ty', 'tx')
The draws below stay inside these ranges and needn't reach their ends.
All inputs are finite; a program needn't handle non-finite values. No bound on the sum of `land_mask` on one device may be relied on, other than what follows from the above.
Results may differ from the reference program's by a relative error of at most 0.00002.
Values sent between devices are 32-bit elements; how exact they have to be, the bound alone decides.
A program may use at most 64 MiB of HBM per device.

```python
import math
import jax
import jax.numpy as jnp
from jax import lax

CONS = 8
NY = 1152
NX = 8192


def with_ends(values, key, least, high):
    index_at = [jax.random.randint(jax.random.fold_in(key, axis), (), 0, length) for axis, length in enumerate(values.shape)]
    widest = values.shape.index(max(values.shape))
    next_to = index_at[:widest] + [(index_at[widest] + 1) % values.shape[widest]] + index_at[widest + 1:]
    return values.at[tuple(index_at)].set(least).at[tuple(next_to)].set(high)


def block_scale(own_key, dims, cuts, smallest, high):
    def one(position, blocks):
        heights = jax.random.uniform(jax.random.fold_in(jax.random.fold_in(own_key, 6), position), (blocks,), jnp.float32, smallest / len(cuts), high / len(cuts))
        return jnp.repeat(jnp.exp(heights), dims[position] // blocks).reshape((-1,) + (1,) * (len(dims) - position - 1))

    level = one(*cuts[0])
    for cut in cuts[1:]:
        level = level * one(*cut)
    return level


def noise(key, shape, spread, most, pieces=(), held_as=jnp.bfloat16):
    drawn = jax.random.normal(key, shape, jnp.float32) * spread
    if len(pieces) > 0:
        drawn = block_scale(key, shape, pieces, -0.22, 0.18) * drawn
    return jnp.clip(drawn, min=-most, max=most).astype(held_as)


def setup_inputs(seed: int = 0) -> dict:
    key_of = jax.random.split(jax.random.key(seed), 6)
    elevation = noise(key_of[0], (CONS, 2, NY, NX), 1.0, 6.0, ((0, 4), (2, 8), (3, 16)), jnp.float32)
    equilibrium = noise(key_of[1], (CONS, 2, NY, NX), 0.7, 5.0, ((0, 4), (2, 8), (3, 16)), jnp.float32)
    depth = jnp.clip(jnp.exp(math.log(1.0) - 2.3025851 * jax.random.uniform(key_of[2], (NY, NX), jnp.float32) ** block_scale(key_of[2], (NY, NX), ((0, 8), (1, 16)), -0.2, 0.2)), 0.1, 1.0)
    land_mask = with_ends((jax.random.randint(key_of[3], (NY, NX), 0, 5) < 4).astype(jnp.int32), jax.random.fold_in(key_of[3], 1), 0, 1)
    friction_prev = jnp.clip(jnp.exp(math.log(3.0) - 2.3025851 * jax.random.uniform(key_of[4], (NY, NX), jnp.float32) ** block_scale(key_of[4], (NY, NX), ((0, 8), (1, 16)), -0.2, 0.2)), 0.3, 3.0)
    return dict(elevation=elevation, equilibrium=equilibrium, depth=depth, land_mask=land_mask, friction_prev=friction_prev)


OMEGA_TABLE = (1.0, 1.0351, 0.9582, 1.0379, 0.5181, 0.4816, 0.5164, 0.4454)
AY_SCALE = 0.5
THETA = 0.05
DRAG = 0.5
BACKGROUND = 0.01

def east_of(field):
    return jnp.roll(field, -1, axis=-1)

def west_of(field):
    return jnp.roll(field, 1, axis=-1)

def north_of(field):
    return jnp.concatenate([field[..., 1:, :], jnp.zeros_like(field[..., :1, :])], axis=-2)

def south_of(field):
    return jnp.concatenate([jnp.zeros_like(field[..., :1, :]), field[..., :-1, :]], axis=-2)

def latitude_factor(rows, total):
    lat = (-60.0 + 120.0 * (rows.astype(jnp.float32) + 0.5) / total) * (math.pi / 180.0)
    return 0.5 / jnp.cos(lat)

def momentum(num_re, num_im, fric, omega, face_mask):
    denom = fric * fric + omega * omega
    return (face_mask * (num_re * fric + num_im * omega) / denom, face_mask * (num_im * fric - num_re * omega) / denom)

def one_sweep(eta, equil, omega, fric, statics):
    ax_rows, maskf, mu_face, mv_face, hu_face, hv_face, depth = statics
    zeta = eta - equil
    grad_x = ax_rows * (east_of(zeta) - zeta)
    grad_y = AY_SCALE * (north_of(zeta) - zeta)
    fric_u = 0.5 * (fric + east_of(fric))
    fric_v = 0.5 * (fric + north_of(fric))
    u_re, u_im = momentum(-hu_face * grad_x[0], -hu_face * grad_x[1], fric_u, omega, mu_face)
    v_re, v_im = momentum(-hv_face * grad_y[0], -hv_face * grad_y[1], fric_v, omega, mv_face)
    trans_u = jnp.stack([u_re, u_im])
    trans_v = jnp.stack([v_re, v_im])
    west_u = west_of(trans_u)
    south_v = south_of(trans_v)
    div = ax_rows * (trans_u - west_u) + AY_SCALE * (trans_v - south_v)
    res = jnp.stack([-omega * eta[1] + div[0], omega * eta[0] + div[1]])
    eta_new = maskf * (eta - THETA * res)
    cu = 0.5 * (trans_u + west_u)
    cv = 0.5 * (trans_v + south_v)
    term = 0.5 * (cu[0] * cu[0] + cu[1] * cu[1] + cv[0] * cv[0] + cv[1] * cv[1]) / (depth * depth)
    return (eta_new, term)

def reference(elevation, equilibrium, depth, land_mask, friction_prev):
    rows = jnp.arange(NY, dtype=jnp.int32)
    ax_rows = latitude_factor(rows, NY)[:, None]
    maskf = land_mask.astype(jnp.float32)
    mu_face = maskf * east_of(maskf)
    mv_face = maskf * north_of(maskf)
    hu_face = 0.5 * (depth + east_of(depth))
    hv_face = 0.5 * (depth + north_of(depth))
    statics = (ax_rows, maskf, mu_face, mv_face, hu_face, hv_face, depth)
    omegas = jnp.array(OMEGA_TABLE, dtype=jnp.float32)

    def first(carry, item):
        eta, equil, omega = item
        eta_new, term = one_sweep(eta, equil, omega, friction_prev, statics)
        return (carry + term, eta_new)
    variance, eta_one = lax.scan(first, jnp.zeros((NY, NX), jnp.float32), (elevation, equilibrium, omegas))
    friction = DRAG * jnp.sqrt(variance + BACKGROUND) / depth

    def second(carry, item):
        eta, equil, omega = item
        eta_new, term = one_sweep(eta, equil, omega, friction, statics)
        return (carry, eta_new)
    unused, eta_two = lax.scan(second, jnp.zeros((), jnp.float32), (eta_one, equilibrium, omegas))
    return (eta_two, friction)
```

```python
import functools
import math

import jax
import jax.numpy as jnp
from jax import lax
from jax.experimental import pallas as pl
from jax.experimental.pallas import tpu as pltpu
from jax.sharding import PartitionSpec as P

OMEGA_TABLE = (1.0, 1.0351, 0.9582, 1.0379, 0.5181, 0.4816, 0.5164, 0.4454)
AY_SCALE = 0.5
THETA = 0.05
DRAG = 0.5
BACKGROUND = 0.01

MESH = pl.DeviceIdType.MESH
LANES = 128
PAD = 8
CHUNKS = 3


def latitude_factor(rows, total):
    lat = (-60.0 + 120.0 * (rows.astype(jnp.float32) + 0.5) / total) * (math.pi / 180.0)
    return 0.5 / jnp.cos(lat)


def rate_of(total, depth):
    inverse = 1.0 / depth
    return DRAG * jnp.sqrt(0.125 * total * (inverse * inverse) + BACKGROUND) * inverse


def face_flow(d_re, d_im, rate, scale, omega):
    along, across = scale * rate, scale * omega
    return along * d_re + across * d_im, along * d_im - across * d_re


def kernel(
    sizes,
    elev, equi, depth_in, mask_in, fric_in,
    out_e, out_f,
    E, Q, D, M, MI, F, AU, AV, V, S, FR, AX, PK, HT, PH,
    row_out, row_in, col_out, col_in,
    ring_out, ring_minus, ring_plus, ring_far,
    rs_minus, rs_plus, rs_far_a, rs_far_b,
    in_sem, halo_send, halo_recv, ring_send, ring_recv, red_send, red_recv,
):
    rows_dev, tiles, n_cons, n_ty, n_tx = sizes
    blocks = rows_dev // 8
    per_chunk = blocks // CHUNKS
    chunk_rows = 8 * per_chunk
    half = chunk_rows // 2
    last_row = PAD + rows_dev
    overlap = rows_dev - LANES

    c = lax.axis_index("cons")
    ty = lax.axis_index("ty")
    tx = lax.axis_index("tx")
    cp, cm, co = lax.rem(c + 1, n_cons), lax.rem(c + n_cons - 1, n_cons), lax.rem(c + 2, n_cons)
    north, south = lax.rem(ty + 1, n_ty), lax.rem(ty + n_ty - 1, n_ty)
    east, west = lax.rem(tx + 1, n_tx), lax.rem(tx + n_tx - 1, n_tx)

    loads = []
    for t in (0, tiles - 1) + tuple(range(1, tiles - 1)):
        lanes = pl.ds(LANES * t, LANES)
        inner = pl.ds(PAD, rows_dev)
        loads += [
            pltpu.make_async_copy(elev.at[:, :, :, lanes], E.at[:, :, t, inner, :], in_sem.at[5 * t]),
            pltpu.make_async_copy(equi.at[:, :, :, lanes], Q.at[:, :, t, inner, :], in_sem.at[5 * t + 1]),
            pltpu.make_async_copy(fric_in.at[:, lanes], F.at[t, inner, :], in_sem.at[5 * t + 2]),
            pltpu.make_async_copy(depth_in.at[:, lanes], D.at[t, inner, :], in_sem.at[5 * t + 3]),
            pltpu.make_async_copy(mask_in.at[:, lanes], MI.at[t], in_sem.at[5 * t + 4]),
        ]
    for load in loads:
        load.start()

    barrier = pltpu.get_barrier_semaphore()
    for there in ({"cons": cp}, {"cons": cm}, {"ty": north}, {"ty": south}, {"tx": east}, {"tx": west}):
        pl.semaphore_signal(barrier, inc=1, device_id=there, device_id_type=MESH)

    omegas = []
    for k in range(2):
        omega = jnp.float32(OMEGA_TABLE[k])
        for group in range(1, n_cons):
            omega = jnp.where(c == group, jnp.float32(OMEGA_TABLE[2 * group + k]), omega)
        omegas.append(omega)

    first_row = ty * rows_dev
    AX[...] = latitude_factor(
        first_row + lax.broadcasted_iota(jnp.int32, (rows_dev, LANES), 0), rows_dev * n_ty
    )
    ax_across = [
        latitude_factor(
            first_row + overlap * h + lax.broadcasted_iota(jnp.int32, (1, LANES), 1), rows_dev * n_ty
        )
        for h in range(2)
    ]

    lane = lax.broadcasted_iota(jnp.int32, (8, LANES), 1)
    lane_0, lane_last = lane == 0, lane == LANES - 1

    for load in loads:
        load.wait()

    @pl.loop(0, blocks)
    def _(b):
        for t in range(tiles):
            M[t, pl.ds(PAD + 8 * b, 8), :] = MI[t, pl.ds(8 * b, 8), :].astype(jnp.float32)

    def plane_of(p, t, rows, extras):
        if p < 4:
            return E[p // 2, p % 2, t, rows, :] - Q[p // 2, p % 2, t, rows, :]
        return extras[p - 4][t, rows, :]

    def pack_columns(extras):
        count = 4 + len(extras)

        @pl.loop(0, blocks)
        def _(b):
            rows = pl.ds(PAD + 8 * b, 8)
            packed = jnp.zeros((8, LANES), jnp.float32)
            for p in range(count):
                first = plane_of(p, 0, rows, extras)
                last = plane_of(p, tiles - 1, rows, extras)
                packed = jnp.where(lane == p, pltpu.roll(first, p, 1) if p else first, packed)
                packed = jnp.where(lane == 8 + p, pltpu.roll(last, 9 + p, 1), packed)
            PK[pl.ds(8 * b, 8), :] = packed

    def transpose_columns(which):
        for h in range(2):
            turned = PK[overlap * h : overlap * h + LANES, :].T
            col_out[which, 0, h] = turned[0:8]
            col_out[which, 1, h] = turned[8:16]

    def pack_rows(which, extras):
        for t in range(tiles):
            for p in range(4 + len(extras)):
                row_out[which, 0, t, p : p + 1, :] = plane_of(p, t, pl.ds(PAD, 1), extras)
                row_out[which, 1, t, p : p + 1, :] = plane_of(p, t, pl.ds(last_row - 1, 1), extras)

    def halo_copies(which):
        copies = []
        for side, (source, target, there) in enumerate(
            (
                (col_out.at[which, 0], col_in.at[which, 1], {"tx": west}),
                (col_out.at[which, 1], col_in.at[which, 0], {"tx": east}),
                (row_out.at[which, 0], row_in.at[which, 1], {"ty": south}),
                (row_out.at[which, 1], row_in.at[which, 0], {"ty": north}),
            )
        ):
            copies.append(
                pltpu.make_async_remote_copy(
                    source, target, halo_send.at[4 * which + side], halo_recv.at[4 * which + side],
                    device_id=there, device_id_type=MESH,
                )
            )
        return copies

    pack_columns((F, D, M))
    transpose_columns(0)
    pack_rows(0, (F, D, M))
    pl.semaphore_wait(barrier, 6)
    halo_one = halo_copies(0)
    for copy in halo_one:
        copy.start()
    for copy in halo_one:
        copy.wait_recv()

    inside_north = jnp.where(ty == n_ty - 1, jnp.float32(0), jnp.float32(1))
    inside_south = jnp.where(ty == 0, jnp.float32(0), jnp.float32(1))
    for t in range(tiles):
        for side, row, keep in ((0, PAD - 1, inside_south), (1, last_row, inside_north)):
            line = pl.ds(row, 1)
            for p in range(4):
                E[p // 2, p % 2, t, line, :] = row_in[0, side, t, p : p + 1, :]
                Q[p // 2, p % 2, t, line, :] = jnp.zeros((1, LANES), jnp.float32)
            F[t, line, :] = row_in[0, side, t, 4:5, :]
            D[t, line, :] = row_in[0, side, t, 5:6, :]
            M[t, line, :] = row_in[0, side, t, 6:7, :] * keep

    def western_flow(h, which, rate):
        own, other = col_out.at[which, 0, h], col_in.at[which, 0, h]
        here, there = col_out.at[0, 0, h], col_in.at[0, 0, h]
        mask = here[6:7, :] * there[6:7, :]
        deep = 0.5 * (here[5:6, :] + there[5:6, :])
        scale = -mask * deep * ax_across[h]
        for k in range(2):
            over = scale / (rate * rate + omegas[k] * omegas[k])
            d_re = own[2 * k : 2 * k + 1, :] - other[2 * k : 2 * k + 1, :]
            d_im = own[2 * k + 1 : 2 * k + 2, :] - other[2 * k + 1 : 2 * k + 2, :]
            u_re, u_im = face_flow(d_re, d_im, rate, over, omegas[k])
            HT[h, 2 * k : 2 * k + 1, :] = u_re
            HT[h, 2 * k + 1 : 2 * k + 2, :] = u_im

    def turn_back():
        PH[0:LANES, :] = HT[0].T
        PH[LANES:rows_dev, :] = HT[1].T[LANES - overlap :]

    for h in range(2):
        HT[h] = jnp.zeros((LANES, LANES), jnp.float32)
        HT[h, 8:16, :] = col_in[0, 1, h]
        western_flow(h, 0, 0.5 * (col_out[0, 0, h, 4:5, :] + col_in[0, 0, h, 4:5, :]))
    turn_back()

    def eastern_views(values, beyond):
        rolled = [pltpu.roll(v, LANES - 1, 1) for v in values] + [beyond]
        return [jnp.where(lane_last, rolled[t + 1], rolled[t]) for t in range(tiles)]

    def both_inverses(ru, rv, au, av, omega):
        square = omega * omega
        du, dv = ru * ru + square, rv * rv + square
        inverse = 1.0 / (du * dv)
        return au * (dv * inverse), av * (du * inverse)

    def southern_flow(R, fresh):
        rows, rows_n = pl.ds(0, 8), pl.ds(1, 8)
        for t in range(tiles):
            if fresh:
                av = -(M[t, rows, :] * M[t, rows_n, :]) * (0.5 * (D[t, rows, :] + D[t, rows_n, :])) * AY_SCALE
                AV[t, rows, :] = av
            else:
                av = AV[t, rows, :]
            rv = 0.5 * (R[t, rows, :] + R[t, rows_n, :])
            for k in range(2):
                over = av / (rv * rv + omegas[k] * omegas[k])
                d = [
                    (E[k, p, t, rows_n, :] - Q[k, p, t, rows_n, :]) - (E[k, p, t, rows, :] - Q[k, p, t, rows, :])
                    for p in range(2)
                ]
                v = face_flow(d[0], d[1], rv, over, omegas[k])
                for p in range(2):
                    V[k, p, t, rows, :] = v[p]

    def sweep_block(b, R, fresh):
        rows, rows_n, rows_s = pl.ds(PAD + 8 * b, 8), pl.ds(PAD + 8 * b + 1, 8), pl.ds(PAD + 8 * b - 1, 8)
        rim = PH[pl.ds(8 * b, 8), :]
        ax = AX[pl.ds(8 * b, 8), :]

        def beyond(p):
            return pltpu.roll(rim, (2 * LANES - 1 - (8 + p)) % LANES, 1)

        rate = [R[t, rows, :] for t in range(tiles)]
        rate_east = eastern_views(rate, beyond(4))
        if fresh:
            deep = [D[t, rows, :] for t in range(tiles)]
            deep_east = eastern_views(deep, beyond(5))
            mask = [M[t, rows, :] for t in range(tiles)]
            mask_east = eastern_views(mask, beyond(6))
        au, av, ru, rv = [], [], [], []
        for t in range(tiles):
            if fresh:
                au.append(-(mask[t] * mask_east[t]) * (0.5 * (deep[t] + deep_east[t])) * ax)
                av.append(-(mask[t] * M[t, rows_n, :]) * (0.5 * (deep[t] + D[t, rows_n, :])) * AY_SCALE)
                AU[t, rows, :] = au[t]
                AV[t, rows, :] = av[t]
            else:
                au.append(AU[t, rows, :])
                av.append(AV[t, rows, :])
            ru.append(0.5 * (rate[t] + rate_east[t]))
            rv.append(0.5 * (rate[t] + R[t, rows_n, :]))
        squares = [None] * tiles
        theta_ax = THETA * ax
        for k in range(2):
            omega = omegas[k]
            eta = [[E[k, p, t, rows, :] for t in range(tiles)] for p in range(2)]
            quil = [[Q[k, p, t, rows, :] for t in range(tiles)] for p in range(2)]
            zeta = [[eta[p][t] - quil[p][t] for t in range(tiles)] for p in range(2)]
            zeta_east = [eastern_views(zeta[p], beyond(2 * k + p)) for p in range(2)]
            flow_u = [[], []]
            flow_v = [[], []]
            for t in range(tiles):
                over_u, over_v = both_inverses(ru[t], rv[t], au[t], av[t], omega)
                u = face_flow(
                    zeta_east[0][t] - zeta[0][t], zeta_east[1][t] - zeta[1][t], ru[t], over_u, omega
                )
                north_z = [E[k, p, t, rows_n, :] - Q[k, p, t, rows_n, :] for p in range(2)]
                v = face_flow(north_z[0] - zeta[0][t], north_z[1] - zeta[1][t], rv[t], over_v, omega)
                for p in range(2):
                    flow_u[p].append(u[p])
                    flow_v[p].append(v[p])
                    V[k, p, t, rows, :] = v[p]
            west_u = []
            for p in range(2):
                q = 2 * k + p
                rolled = [pltpu.roll(rim, LANES - q, 1) if q else rim]
                rolled += [pltpu.roll(flow_u[p][t], 1, 1) for t in range(tiles)]
                west_u.append([jnp.where(lane_0, rolled[t], rolled[t + 1]) for t in range(tiles)])
            for t in range(tiles):
                south_v = [V[k, p, t, rows_s, :] for p in range(2)]
                for p in range(2):
                    turning = -omega * eta[1][t] if p == 0 else omega * eta[0][t]
                    change = (
                        THETA * turning
                        + theta_ax * (flow_u[p][t] - west_u[p][t])
                        + (THETA * AY_SCALE) * (flow_v[p][t] - south_v[p])
                    )
                    new = M[t, rows, :] * (eta[p][t] - change)
                    if fresh:
                        E[k, p, t, rows, :] = new
                        cu = flow_u[p][t] + west_u[p][t]
                        cv = flow_v[p][t] + south_v[p]
                        term = cu * cu + cv * cv
                        squares[t] = term if squares[t] is None else squares[t] + term
                    else:
                        out_e[k, p, pl.ds(8 * b, 8), LANES * t : LANES * (t + 1)] = new
        for t in range(tiles):
            if fresh:
                S[t, rows, :] = squares[t]
            else:
                out_f[pl.ds(8 * b, 8), LANES * t : LANES * (t + 1)] = rate[t]

    def span(j, part):
        start = PAD + chunk_rows * j
        if part == "a":
            return pl.ds(start, half)
        if part == "b":
            return pl.ds(start + half, half)
        return pl.ds(start, chunk_rows)

    def buffer_span(j):
        return pl.ds(half * j, half)

    def remote(source, target, slot, there):
        return pltpu.make_async_remote_copy(
            source, target, red_send.at[slot], red_recv.at[slot], device_id={"cons": there}, device_id_type=MESH
        )

    sent = []
    far, near, gather, relay = {}, {}, {}, {}

    def reduce_first(j):
        far[j] = (
            remote(S.at[co, span(j, "a"), :], rs_far_a.at[buffer_span(j), :], 10 * j, cp),
            remote(S.at[co, span(j, "b"), :], rs_far_b.at[buffer_span(j), :], 10 * j + 1, cm),
        )
        near[j] = (
            remote(S.at[cp, span(j, "b"), :], rs_minus.at[1, buffer_span(j), :], 10 * j + 2, cp),
            remote(S.at[cm, span(j, "a"), :], rs_plus.at[0, buffer_span(j), :], 10 * j + 3, cm),
        )
        for copy in far[j] + near[j]:
            copy.start()

    def reduce_second(j):
        far[j][0].wait_recv()
        rs_far_a[buffer_span(j), :] = S[cp, span(j, "a"), :] + rs_far_a[buffer_span(j), :]
        far[j][1].wait_recv()
        rs_far_b[buffer_span(j), :] = S[cm, span(j, "b"), :] + rs_far_b[buffer_span(j), :]
        near[j] += (
            remote(rs_far_a.at[buffer_span(j), :], rs_minus.at[0, buffer_span(j), :], 10 * j + 4, cp),
            remote(rs_far_b.at[buffer_span(j), :], rs_plus.at[1, buffer_span(j), :], 10 * j + 5, cm),
        )
        for copy in near[j][2:]:
            copy.start()

    def gather_first(j):
        for copy in near[j]:
            copy.wait_recv()
        for h, part in enumerate("ab"):
            rows = span(j, part)
            total = S[c, rows, :] + rs_minus[h, buffer_span(j), :] + rs_plus[h, buffer_span(j), :]
            FR[c, rows, :] = rate_of(total, D[c, rows, :])
        gather[j] = (
            remote(FR.at[c, span(j, ""), :], FR.at[c, span(j, ""), :], 10 * j + 6, cp),
            remote(FR.at[c, span(j, ""), :], FR.at[c, span(j, ""), :], 10 * j + 7, cm),
        )
        for copy in gather[j]:
            copy.start()

    def gather_second(j):
        for copy in gather[j]:
            copy.wait_recv()
        relay[j] = (
            remote(FR.at[cm, span(j, "a"), :], FR.at[cm, span(j, "a"), :], 10 * j + 8, cp),
            remote(FR.at[cp, span(j, "b"), :], FR.at[cp, span(j, "b"), :], 10 * j + 9, cm),
        )
        for copy in relay[j]:
            copy.start()

    def gathered(j):
        for copy in relay[j]:
            copy.wait_recv()

    southern_flow(F, True)
    for j in range(CHUNKS):

        @pl.loop(per_chunk * j, per_chunk * (j + 1))
        def _(b):
            sweep_block(b, F, True)

        reduce_first(j)
        if j >= 1:
            reduce_second(j - 1)
        if j >= 2:
            gather_first(j - 2)

    pack_columns((S,))
    transpose_columns(1)
    pack_rows(1, (S,))
    halo_two = halo_copies(1)
    for copy in halo_two:
        copy.start()

    reduce_second(CHUNKS - 1)
    gather_first(CHUNKS - 2)
    for copy in halo_two:
        copy.wait_recv()
    for t in range(tiles):
        ring_out[t : t + 1, :] = row_in[1, 0, t, 4:5, :]
        ring_out[tiles + t : tiles + t + 1, :] = row_in[1, 1, t, 4:5, :]
    for h in range(2):
        ring_out[8 + h : 9 + h, :] = col_in[1, 0, h, 4:5, :]
        ring_out[10 + h : 11 + h, :] = col_in[1, 1, h, 4:5, :]
        ring_out[12 + h : 13 + h, :] = col_out[1, 0, h, 4:5, :]
    ring_out[14:16, :] = jnp.zeros((2, LANES), jnp.float32)

    def ring_remote(source, target, slot, there):
        return pltpu.make_async_remote_copy(
            source, target, ring_send.at[slot], ring_recv.at[slot], device_id={"cons": there}, device_id_type=MESH
        )

    ring = [ring_remote(ring_out, ring_minus, 0, cp), ring_remote(ring_out, ring_plus, 1, cm)]
    for copy in ring:
        copy.start()
    gather_first(CHUNKS - 1)
    ring[0].wait_recv()
    ring.append(ring_remote(ring_minus, ring_far, 2, cp))
    ring[2].start()
    for j in range(CHUNKS):
        gather_second(j)
    ring[1].wait_recv()
    ring[2].wait_recv()

    def ring_rate(line, depth):
        rows = slice(line, line + 1)
        total = (ring_out[rows, :] + ring_minus[rows, :]) + (ring_plus[rows, :] + ring_far[rows, :])
        return rate_of(total, depth)

    for t in range(tiles):
        for side, row in ((0, PAD - 1), (1, last_row)):
            line = pl.ds(row, 1)
            for p in range(4):
                E[p // 2, p % 2, t, line, :] = row_in[1, side, t, p : p + 1, :]
            FR[t, line, :] = ring_rate(tiles * side + t, row_in[0, side, t, 5:6, :])
    for h in range(2):
        rate_west = ring_rate(8 + h, col_in[0, 0, h, 5:6, :])
        rate_east = ring_rate(10 + h, col_in[0, 1, h, 5:6, :])
        rate_own = ring_rate(12 + h, col_out[0, 0, h, 5:6, :])
        HT[h, 8:12, :] = col_in[1, 1, h, 0:4, :]
        HT[h, 12:13, :] = rate_east
        western_flow(h, 1, 0.5 * (rate_own + rate_west))
    turn_back()

    gathered(0)
    southern_flow(FR, False)
    for j in range(CHUNKS):
        if j + 1 < CHUNKS:
            gathered(j + 1)

        @pl.loop(per_chunk * j, per_chunk * (j + 1))
        def _(b):
            sweep_block(b, FR, False)

    for copy in halo_one + halo_two + ring:
        copy.wait_send()
    for j in range(CHUNKS):
        for copy in far[j] + near[j] + gather[j] + relay[j]:
            copy.wait_send()


def solution(mesh):
    n_cons, n_ty, n_tx = (mesh.shape[axis] for axis in ("cons", "ty", "tx"))

    def body(elevation, equilibrium, depth, land_mask, friction_prev):
        kdev, two, rows_dev, cols_dev = elevation.shape
        tiles = cols_dev // LANES
        tall = rows_dev + 2 * PAD
        f32 = jnp.float32
        field = pltpu.VMEM((tiles, tall, LANES), f32)
        fields = pltpu.VMEM((2, 2, tiles, tall, LANES), f32)
        half_rows = rows_dev // 2
        hbm = pl.BlockSpec(memory_space=pltpu.HBM)
        vmem = pl.BlockSpec(memory_space=pltpu.VMEM)
        return pl.pallas_call(
            functools.partial(kernel, (rows_dev, tiles, n_cons, n_ty, n_tx)),
            out_shape=(
                jax.ShapeDtypeStruct(elevation.shape, f32),
                jax.ShapeDtypeStruct(depth.shape, f32),
            ),
            in_specs=[hbm] * 5,
            out_specs=(vmem, vmem),
            scratch_shapes=[
                fields, fields, field, field,
                pltpu.VMEM((tiles, rows_dev, LANES), jnp.int32),
                field, field, field, fields, field, field,
                pltpu.VMEM((rows_dev, LANES), f32),
                pltpu.VMEM((rows_dev, LANES), f32),
                pltpu.VMEM((2, LANES, LANES), f32),
                pltpu.VMEM((rows_dev, LANES), f32),
                pltpu.VMEM((2, 2, tiles, 8, LANES), f32),
                pltpu.VMEM((2, 2, tiles, 8, LANES), f32),
                pltpu.VMEM((2, 2, 2, 8, LANES), f32),
                pltpu.VMEM((2, 2, 2, 8, LANES), f32),
                pltpu.VMEM((16, LANES), f32),
                pltpu.VMEM((16, LANES), f32),
                pltpu.VMEM((16, LANES), f32),
                pltpu.VMEM((16, LANES), f32),
                pltpu.VMEM((2, half_rows, LANES), f32),
                pltpu.VMEM((2, half_rows, LANES), f32),
                pltpu.VMEM((half_rows, LANES), f32),
                pltpu.VMEM((half_rows, LANES), f32),
                pltpu.SemaphoreType.DMA((5 * tiles,)),
                pltpu.SemaphoreType.DMA((8,)),
                pltpu.SemaphoreType.DMA((8,)),
                pltpu.SemaphoreType.DMA((3,)),
                pltpu.SemaphoreType.DMA((3,)),
                pltpu.SemaphoreType.DMA((10 * CHUNKS,)),
                pltpu.SemaphoreType.DMA((10 * CHUNKS,)),
            ],
            compiler_params=pltpu.CompilerParams(collective_id=0, has_side_effects=True),
        )(elevation, equilibrium, depth, land_mask, friction_prev)

    tiled = P("ty", "tx")
    planes = P("cons", None, "ty", "tx")
    return jax.shard_map(
        body,
        mesh=mesh,
        in_specs=(planes, planes, tiled, tiled, tiled),
        out_specs=(planes, tiled),
        check_vma=False,
    )
```

```python
import functools
import math

import jax
import jax.numpy as jnp
from jax import lax
from jax.experimental import pallas as pl
from jax.experimental.pallas import tpu as pltpu
from jax.sharding import PartitionSpec as P

OMEGA_TABLE = (1.0, 1.0351, 0.9582, 1.0379, 0.5181, 0.4816, 0.5164, 0.4454)
AY_SCALE = 0.5
THETA = 0.05
DRAG = 0.5
BACKGROUND = 0.01

MESH = pl.DeviceIdType.MESH
LANES = 128
PAD = 8
FAR_FIRST = (2, 1, 3)
INNER = ((1, 9), (9, 17))
OUTER = ((0, 12), (12, 18))


def latitude_factor(rows, total):
    lat = (-60.0 + 120.0 * (rows.astype(jnp.float32) + 0.5) / total) * (math.pi / 180.0)
    return 0.5 / jnp.cos(lat)


def rate_of(total, depth):
    inverse = 1.0 / depth
    return DRAG * jnp.sqrt(0.125 * total * (inverse * inverse) + BACKGROUND) * inverse


def face_flow(d_re, d_im, rate, scale, omega):
    along, across = scale * rate, scale * omega
    return along * d_re + across * d_im, along * d_im - across * d_re


def kernel(
    sizes,
    elev, equi, depth_in, mask_in, fric_in,
    out_e, out_f,
    E, Q, E1, D, M, MI, F, AU, AV, U0, U2, V, S, FR, AX, PK, HT, PH,
    row_out, row_in, col_out, col_in, ring_out, ring_in, part_in,
    in_sem, halo_send, halo_recv, ring_send, ring_recv, part_send, part_recv, rate_send, rate_recv,
):
    rows_dev, tiles, n_cons, n_ty, n_tx = sizes
    blocks = rows_dev // 8
    last_row = PAD + rows_dev
    overlap = rows_dev - LANES
    inner_tiles, outer_tiles = tuple(range(1, tiles - 1)), (0, tiles - 1)

    c = lax.axis_index("cons")
    ty = lax.axis_index("ty")
    tx = lax.axis_index("tx")
    others = [lax.rem(c + d, n_cons) for d in range(1, n_cons)]
    owners = [lax.rem(c + n_cons - d, n_cons) for d in range(1, n_cons)]
    north, south = lax.rem(ty + 1, n_ty), lax.rem(ty + n_ty - 1, n_ty)
    east, west = lax.rem(tx + 1, n_tx), lax.rem(tx + n_tx - 1, n_tx)

    loads = []
    for t in outer_tiles + inner_tiles:
        lanes = pl.ds(LANES * t, LANES)
        within = pl.ds(PAD, rows_dev)
        loads += [
            pltpu.make_async_copy(elev.at[:, :, :, lanes], E.at[:, :, t, within, :], in_sem.at[5 * t]),
            pltpu.make_async_copy(equi.at[:, :, :, lanes], Q.at[:, :, t, within, :], in_sem.at[5 * t + 1]),
            pltpu.make_async_copy(fric_in.at[:, lanes], F.at[t, within, :], in_sem.at[5 * t + 2]),
            pltpu.make_async_copy(depth_in.at[:, lanes], D.at[t, within, :], in_sem.at[5 * t + 3]),
            pltpu.make_async_copy(mask_in.at[:, lanes], MI.at[t], in_sem.at[5 * t + 4]),
        ]
    for load in loads:
        load.start()

    barrier = pltpu.get_barrier_semaphore()
    met = [{"cons": other} for other in others]
    met += [{"ty": north}, {"ty": south}, {"tx": east}, {"tx": west}]
    for there in met:
        pl.semaphore_signal(barrier, inc=1, device_id=there, device_id_type=MESH)

    omegas = []
    for k in range(2):
        omega = jnp.float32(OMEGA_TABLE[k])
        for group in range(1, n_cons):
            omega = jnp.where(c == group, jnp.float32(OMEGA_TABLE[2 * group + k]), omega)
        omegas.append(omega)

    first_row = ty * rows_dev
    AX[...] = latitude_factor(
        first_row + lax.broadcasted_iota(jnp.int32, (rows_dev, LANES), 0), rows_dev * n_ty
    )
    ax_across = [
        latitude_factor(
            first_row + overlap * h + lax.broadcasted_iota(jnp.int32, (1, LANES), 1), rows_dev * n_ty
        )
        for h in range(2)
    ]

    lane = lax.broadcasted_iota(jnp.int32, (8, LANES), 1)
    lane_0, lane_last = lane == 0, lane == LANES - 1

    def arrive(tiles_now, copies):
        for load in copies:
            load.wait()

        @pl.loop(0, blocks, unroll=6)
        def _(b):
            for t in tiles_now:
                M[t, pl.ds(PAD + 8 * b, 8), :] = MI[t, pl.ds(8 * b, 8), :].astype(jnp.float32)

    arrive(outer_tiles, loads[:10])

    def plane_of(p, t, rows, eta, extras):
        if p < 4:
            return eta[p // 2, p % 2, t, rows, :] - Q[p // 2, p % 2, t, rows, :]
        return extras[p - 4][t, rows, :]

    def pack_columns(which, eta, extras):
        @pl.loop(0, blocks, unroll=6)
        def _(b):
            rows = pl.ds(PAD + 8 * b, 8)
            packed = jnp.zeros((8, LANES), jnp.float32)
            for p in range(4 + len(extras)):
                first = plane_of(p, 0, rows, eta, extras)
                last = plane_of(p, tiles - 1, rows, eta, extras)
                packed = jnp.where(lane == p, pltpu.roll(first, p, 1) if p else first, packed)
                packed = jnp.where(lane == 8 + p, pltpu.roll(last, 9 + p, 1), packed)
            PK[pl.ds(8 * b, 8), :] = packed

        for h in range(2):
            turned = PK[overlap * h : overlap * h + LANES, :].T
            col_out[which, 0, h] = turned[0:8]
            col_out[which, 1, h] = turned[8:16]

    def pack_rows(which, eta, extras):
        for t in range(tiles):
            for p in range(4 + len(extras)):
                row_out[which, 0, t, p : p + 1, :] = plane_of(p, t, pl.ds(PAD, 1), eta, extras)
                row_out[which, 1, t, p : p + 1, :] = plane_of(p, t, pl.ds(last_row - 1, 1), eta, extras)

    def halo_copies(which):
        copies = []
        for side, (source, target, there) in enumerate(
            (
                (col_out.at[which, 0], col_in.at[which, 1], {"tx": west}),
                (col_out.at[which, 1], col_in.at[which, 0], {"tx": east}),
                (row_out.at[which, 0], row_in.at[which, 1], {"ty": south}),
                (row_out.at[which, 1], row_in.at[which, 0], {"ty": north}),
            )
        ):
            copies.append(
                pltpu.make_async_remote_copy(
                    source, target, halo_send.at[4 * which + side], halo_recv.at[4 * which + side],
                    device_id=there, device_id_type=MESH,
                )
            )
        return copies

    groups = [(inner_tiles, a, (b - a) // 2, (b - a) // 2) for a, b in INNER] + [(inner_tiles, 0, 1, blocks - 1)]
    groups += [(outer_tiles, a, (b - a) // 2, (b - a) // 2) for a, b in OUTER]
    edges = len(INNER)

    def piece(g, owner):
        pair, first, count, step = groups[g]
        tile = pair[0] + (pair[1] - pair[0]) * (owner // 2)
        start = PAD + 8 * first + (8 * step) * lax.rem(owner, 2)
        return tile, pl.ds(pl.multiple_of(start, 8), 8 * count)

    def landing(g):
        start = 8 * sum(group[2] for group in groups[:g])
        return pl.ds(start, 8 * groups[g][2])

    def part_copy(g, d):
        tile, rows = piece(g, others[d - 1])
        return pltpu.make_async_remote_copy(
            S.at[tile, rows, :], part_in.at[d - 1, landing(g), :],
            part_send.at[g, d - 1], part_recv.at[g, d - 1],
            device_id={"cons": others[d - 1]}, device_id_type=MESH,
        )

    def rate_copy(g, d, source):
        tile, rows = piece(g, source)
        return pltpu.make_async_remote_copy(
            FR.at[tile, rows, :], FR.at[tile, rows, :],
            rate_send.at[g, d - 1], rate_recv.at[g, d - 1],
            device_id={"cons": others[d - 1]}, device_id_type=MESH,
        )

    def send_parts(g):
        for d in FAR_FIRST:
            part_copy(g, d).start()

    def settle(g):
        for d in FAR_FIRST:
            part_copy(g, d).wait_recv()
        tile, rows = piece(g, c)
        total = S[tile, rows, :]
        for d in FAR_FIRST:
            total = total + part_in[d - 1, landing(g), :]
        FR[tile, rows, :] = rate_of(total, D[tile, rows, :])
        for d in FAR_FIRST:
            rate_copy(g, d, c).start()

    def gathered(g):
        for d in FAR_FIRST:
            rate_copy(g, d, owners[d - 1]).wait_recv()

    def faces(mask, mask_next, deep, deep_next, scale):
        return -(mask * mask_next) * (0.5 * (deep + deep_next)) * scale

    def both_inverses(ru, rv, au, av, omega):
        square = omega * omega
        du, dv = ru * ru + square, rv * rv + square
        inverse = 1.0 / (du * dv)
        return au * (dv * inverse), av * (du * inverse)

    def northward(R, eta, fresh, start, which_tiles):
        rows, rows_n = pl.ds(start, 8), pl.ds(start + 1, 8)
        for t in which_tiles:
            if fresh:
                av = faces(M[t, rows, :], M[t, rows_n, :], D[t, rows, :], D[t, rows_n, :], AY_SCALE)
                AV[t, rows, :] = av
            else:
                av = AV[t, rows, :]
            rv = 0.5 * (R[t, rows, :] + R[t, rows_n, :])
            for k in range(2):
                over = av / (rv * rv + omegas[k] * omegas[k])
                d = [
                    (eta[k, p, t, rows_n, :] - Q[k, p, t, rows_n, :]) - (eta[k, p, t, rows, :] - Q[k, p, t, rows, :])
                    for p in range(2)
                ]
                v = face_flow(d[0], d[1], rv, over, omegas[k])
                for p in range(2):
                    V[k, p, t, rows, :] = v[p]

    def half_sweep(b, R, eta, fresh, inner):
        rows, rows_n, rows_s = pl.ds(PAD + 8 * b, 8), pl.ds(PAD + 8 * b + 1, 8), pl.ds(PAD + 8 * b - 1, 8)
        ax = AX[pl.ds(8 * b, 8), :]
        flowing = tuple(range(tiles - 1)) if inner else (tiles - 1,)
        closing = inner_tiles if inner else outer_tiles
        rim = None if inner else PH[pl.ds(8 * b, 8), :]

        def views(load, p):
            values = {t: load(t) for t in flowing}
            rolled = {t: pltpu.roll(values[t], LANES - 1, 1) for t in flowing}
            if inner:
                rolled[tiles - 1] = pltpu.roll(load(tiles - 1), LANES - 1, 1)
            else:
                rolled[tiles] = pltpu.roll(rim, (2 * LANES - 1 - (8 + p)) % LANES, 1)
            return values, {t: jnp.where(lane_last, rolled[t + 1], rolled[t]) for t in flowing}

        rate, rate_east = views(lambda t: R[t, rows, :], 4)
        if fresh:
            deep, deep_east = views(lambda t: D[t, rows, :], 5)
            mask, mask_east = views(lambda t: M[t, rows, :], 6)
        au, av, ru, rv = {}, {}, {}, {}
        for t in flowing:
            if fresh:
                au[t] = faces(mask[t], mask_east[t], deep[t], deep_east[t], ax)
                av[t] = faces(mask[t], M[t, rows_n, :], deep[t], D[t, rows_n, :], AY_SCALE)
                AU[t, rows, :] = au[t]
                AV[t, rows, :] = av[t]
            else:
                au[t] = AU[t, rows, :]
                av[t] = AV[t, rows, :]
            ru[t] = 0.5 * (rate[t] + rate_east[t])
            rv[t] = 0.5 * (rate[t] + R[t, rows_n, :])
        squares = {t: None for t in closing}
        theta_ax = THETA * ax
        for k in range(2):
            omega = omegas[k]
            theta_omega = THETA * omega
            zeta, zeta_east = [None, None], [None, None]
            for p in range(2):
                zeta[p], zeta_east[p] = views(lambda t: eta[k, p, t, rows, :] - Q[k, p, t, rows, :], 2 * k + p)
            flow_u, flow_v = [{}, {}], [{}, {}]
            for t in flowing:
                over_u, over_v = both_inverses(ru[t], rv[t], au[t], av[t], omega)
                u = face_flow(
                    zeta_east[0][t] - zeta[0][t], zeta_east[1][t] - zeta[1][t], ru[t], over_u, omega
                )
                north_z = [eta[k, p, t, rows_n, :] - Q[k, p, t, rows_n, :] for p in range(2)]
                v = face_flow(north_z[0] - zeta[0][t], north_z[1] - zeta[1][t], rv[t], over_v, omega)
                for p in range(2):
                    flow_u[p][t], flow_v[p][t] = u[p], v[p]
                    V[k, p, t, rows, :] = v[p]
            west_u = [{}, {}]
            for p in range(2):
                if inner:
                    rolled = {t: pltpu.roll(flow_u[p][t], 1, 1) for t in flowing}
                    U0[k, p, pl.ds(8 * b, 8), :] = flow_u[p][0]
                    U2[k, p, pl.ds(8 * b, 8), :] = rolled[tiles - 2]
                else:
                    q = 2 * k + p
                    flow_u[p][0] = U0[k, p, pl.ds(8 * b, 8), :]
                    flow_v[p][0] = V[k, p, 0, rows, :]
                    rolled = {t: pltpu.roll(flow_u[p][t], 1, 1) for t in closing}
                    rolled[-1] = pltpu.roll(rim, LANES - q, 1) if q else rim
                    rolled[tiles - 2] = U2[k, p, pl.ds(8 * b, 8), :]
                for t in closing:
                    west_u[p][t] = jnp.where(lane_0, rolled[t - 1], rolled[t])
            for t in closing:
                old = [eta[k, p, t, rows, :] for p in range(2)]
                wet = M[t, rows, :]
                for p in range(2):
                    south_v = V[k, p, t, rows_s, :]
                    turned = old[p] + theta_omega * old[1] if p == 0 else old[p] - theta_omega * old[0]
                    new = wet * (
                        turned
                        - theta_ax * (flow_u[p][t] - west_u[p][t])
                        - (THETA * AY_SCALE) * (flow_v[p][t] - south_v)
                    )
                    if fresh:
                        E1[k, p, t, rows, :] = new
                        cu = flow_u[p][t] + west_u[p][t]
                        cv = flow_v[p][t] + south_v
                        term = cu * cu + cv * cv
                        squares[t] = term if squares[t] is None else squares[t] + term
                    else:
                        out_e[k, p, pl.ds(8 * b, 8), LANES * t : LANES * (t + 1)] = new
        for t in closing:
            if fresh:
                S[t, rows, :] = squares[t]
            else:
                out_f[pl.ds(8 * b, 8), LANES * t : LANES * (t + 1)] = R[t, rows, :]

    def run(span, R, eta, fresh, inner):
        @pl.loop(span[0], span[1], unroll=next(u for u in (4, 3, 5, 2, 1) if (span[1] - span[0]) % u == 0))
        def _(b):
            half_sweep(b, R, eta, fresh, inner)

    pack_columns(0, E, (F, D, M))
    arrive(inner_tiles, loads[10:])
    pack_rows(0, E, (F, D, M))
    pl.semaphore_wait(barrier, len(met))
    halo_one = halo_copies(0)
    for copy in halo_one:
        copy.start()
    northward(F, E, True, PAD, inner_tiles)
    for g in (0, 1):
        run(INNER[g], F, E, True, True)
        send_parts(g)
    for copy in halo_one:
        copy.wait_recv()

    inside_north = jnp.where(ty == n_ty - 1, jnp.float32(0), jnp.float32(1))
    inside_south = jnp.where(ty == 0, jnp.float32(0), jnp.float32(1))
    for t in range(tiles):
        for side, row, keep in ((0, PAD - 1, inside_south), (1, last_row, inside_north)):
            line = pl.ds(row, 1)
            for p in range(4):
                E[p // 2, p % 2, t, line, :] = row_in[0, side, t, p : p + 1, :]
                Q[p // 2, p % 2, t, line, :] = jnp.zeros((1, LANES), jnp.float32)
            F[t, line, :] = row_in[0, side, t, 4:5, :]
            D[t, line, :] = row_in[0, side, t, 5:6, :]
            M[t, line, :] = row_in[0, side, t, 6:7, :] * keep

    def western_flow(h, which, rate):
        own, other = col_out.at[which, 0, h], col_in.at[which, 0, h]
        here, there = col_out.at[0, 0, h], col_in.at[0, 0, h]
        scale = faces(here[6:7, :], there[6:7, :], here[5:6, :], there[5:6, :], ax_across[h])
        for k in range(2):
            over = scale / (rate * rate + omegas[k] * omegas[k])
            d_re = own[2 * k : 2 * k + 1, :] - other[2 * k : 2 * k + 1, :]
            d_im = own[2 * k + 1 : 2 * k + 2, :] - other[2 * k + 1 : 2 * k + 2, :]
            u_re, u_im = face_flow(d_re, d_im, rate, over, omegas[k])
            HT[h, 2 * k : 2 * k + 1, :] = u_re
            HT[h, 2 * k + 1 : 2 * k + 2, :] = u_im

    def turn_back():
        PH[0:LANES, :] = HT[0].T
        PH[LANES:rows_dev, :] = HT[1].T[LANES - overlap :]

    for h in range(2):
        HT[h] = jnp.zeros((LANES, LANES), jnp.float32)
        HT[h, 8:16, :] = col_in[0, 1, h]
        western_flow(h, 0, 0.5 * (col_out[0, 0, h, 4:5, :] + col_in[0, 0, h, 4:5, :]))
    turn_back()
    northward(F, E, True, 0, range(tiles))
    for b in (0, blocks - 1):
        half_sweep(b, F, E, True, True)
    send_parts(edges)
    first_outer = edges + 1
    for i, span in enumerate(OUTER):
        run(span, F, E, True, False)
        send_parts(first_outer + i)

    pack_columns(1, E1, (S,))
    pack_rows(1, E1, (S,))
    halo_two = halo_copies(1)
    for copy in halo_two:
        copy.start()
    for g in range(first_outer):
        settle(g)
    settle(first_outer)
    for copy in halo_two:
        copy.wait_recv()
    for t in range(tiles):
        ring_out[t : t + 1, :] = row_in[1, 0, t, 4:5, :]
        ring_out[tiles + t : tiles + t + 1, :] = row_in[1, 1, t, 4:5, :]
    for h in range(2):
        ring_out[8 + h : 9 + h, :] = col_in[1, 0, h, 4:5, :]
        ring_out[10 + h : 11 + h, :] = col_in[1, 1, h, 4:5, :]
        ring_out[12 + h : 13 + h, :] = col_out[1, 0, h, 4:5, :]
    ring_out[14:16, :] = jnp.zeros((2, LANES), jnp.float32)
    ring = [
        pltpu.make_async_remote_copy(
            ring_out, ring_in.at[d - 1], ring_send.at[d - 1], ring_recv.at[d - 1],
            device_id={"cons": others[d - 1]}, device_id_type=MESH,
        )
        for d in range(1, n_cons)
    ]
    for copy in ring:
        copy.start()
    for g in range(first_outer + 1, len(groups)):
        settle(g)

    for g in (0, edges, first_outer):
        gathered(g)
    northward(FR, E1, False, PAD, inner_tiles)
    gathered(1)
    run((1, 11), FR, E1, False, True)
    gathered(first_outer + 1)
    run((11, 17), FR, E1, False, True)

    for copy in ring:
        copy.wait_recv()

    def ring_rate(line, depth):
        rows = slice(line, line + 1)
        total = (ring_out[rows, :] + ring_in[0, rows, :]) + (ring_in[1, rows, :] + ring_in[2, rows, :])
        return rate_of(total, depth)

    for t in range(tiles):
        for side, row in ((0, PAD - 1), (1, last_row)):
            line = pl.ds(row, 1)
            for p in range(4):
                E1[p // 2, p % 2, t, line, :] = row_in[1, side, t, p : p + 1, :]
            FR[t, line, :] = ring_rate(tiles * side + t, row_in[0, side, t, 5:6, :])
    for h in range(2):
        rate_west = ring_rate(8 + h, col_in[0, 0, h, 5:6, :])
        rate_east = ring_rate(10 + h, col_in[0, 1, h, 5:6, :])
        rate_own = ring_rate(12 + h, col_out[0, 0, h, 5:6, :])
        HT[h, 8:12, :] = col_in[1, 1, h, 0:4, :]
        HT[h, 12:13, :] = rate_east
        western_flow(h, 1, 0.5 * (rate_own + rate_west))
    turn_back()
    northward(FR, E1, False, 0, range(tiles))
    for b in (0, blocks - 1):
        half_sweep(b, FR, E1, False, True)
    run((0, blocks), FR, E1, False, False)

    for copy in halo_one + halo_two + ring:
        copy.wait_send()
    for g in range(len(groups)):
        for d in FAR_FIRST:
            part_copy(g, d).wait_send()
            rate_copy(g, d, c).wait_send()


def solution(mesh):
    n_cons, n_ty, n_tx = (mesh.shape[axis] for axis in ("cons", "ty", "tx"))

    def body(elevation, equilibrium, depth, land_mask, friction_prev):
        kdev, two, rows_dev, cols_dev = elevation.shape
        tiles = cols_dev // LANES
        tall = rows_dev + 2 * PAD
        f32 = jnp.float32
        field = pltpu.VMEM((tiles, tall, LANES), f32)
        fields = pltpu.VMEM((2, 2, tiles, tall, LANES), f32)
        n_groups = len(INNER) + len(OUTER) + 1
        hbm = pl.BlockSpec(memory_space=pltpu.HBM)
        vmem = pl.BlockSpec(memory_space=pltpu.VMEM)
        return pl.pallas_call(
            functools.partial(kernel, (rows_dev, tiles, n_cons, n_ty, n_tx)),
            out_shape=(
                pltpu.VMEM(elevation.shape, f32),
                pltpu.VMEM(depth.shape, f32),
            ),
            in_specs=[hbm] * 5,
            out_specs=(vmem, vmem),
            scratch_shapes=[
                fields, fields, fields, field, field,
                pltpu.VMEM((tiles, rows_dev, LANES), jnp.int32),
                field, field, field,
                pltpu.VMEM((2, 2, rows_dev, LANES), f32),
                pltpu.VMEM((2, 2, rows_dev, LANES), f32),
                fields, field, field,
                pltpu.VMEM((rows_dev, LANES), f32),
                pltpu.VMEM((rows_dev, LANES), f32),
                pltpu.VMEM((2, LANES, LANES), f32),
                pltpu.VMEM((rows_dev, LANES), f32),
                pltpu.VMEM((2, 2, tiles, 8, LANES), f32),
                pltpu.VMEM((2, 2, tiles, 8, LANES), f32),
                pltpu.VMEM((2, 2, 2, 8, LANES), f32),
                pltpu.VMEM((2, 2, 2, 8, LANES), f32),
                pltpu.VMEM((16, LANES), f32),
                pltpu.VMEM((n_cons - 1, 16, LANES), f32),
                pltpu.VMEM((n_cons - 1, rows_dev, LANES), f32),
                pltpu.SemaphoreType.DMA((5 * tiles,)),
                pltpu.SemaphoreType.DMA((8,)),
                pltpu.SemaphoreType.DMA((8,)),
                pltpu.SemaphoreType.DMA((n_cons - 1,)),
                pltpu.SemaphoreType.DMA((n_cons - 1,)),
                pltpu.SemaphoreType.DMA((n_groups, n_cons - 1)),
                pltpu.SemaphoreType.DMA((n_groups, n_cons - 1)),
                pltpu.SemaphoreType.DMA((n_groups, n_cons - 1)),
                pltpu.SemaphoreType.DMA((n_groups, n_cons - 1)),
            ],
            compiler_params=pltpu.CompilerParams(collective_id=0, has_side_effects=True, vmem_limit_bytes=56 * 2**20),
        )(elevation, equilibrium, depth, land_mask, friction_prev)

    tiled = P("ty", "tx")
    planes = P("cons", None, "ty", "tx")
    return jax.shard_map(
        body,
        mesh=mesh,
        in_specs=(planes, planes, tiled, tiled, tiled),
        out_specs=(planes, tiled),
        check_vma=False,
    )
```

```python
import functools
import math

import jax
import jax.numpy as jnp
from jax import lax
from jax.experimental import pallas as pl
from jax.experimental.pallas import tpu as pltpu
from jax.sharding import PartitionSpec as P

OMEGA_TABLE = (1.0, 1.0351, 0.9582, 1.0379, 0.5181, 0.4816, 0.5164, 0.4454)
AY_SCALE = 0.5
THETA = 0.05
DRAG = 0.5
BACKGROUND = 0.01

MESH = pl.DeviceIdType.MESH
LANES = 128
PAD = 8
FAR_FIRST = (2, 1, 3)
INNER = ((1, 9), (9, 17))
OUTER = ((0, 12), (12, 18))


def latitude_factor(rows, total):
    lat = (-60.0 + 120.0 * (rows.astype(jnp.float32) + 0.5) / total) * (math.pi / 180.0)
    return 0.5 / jnp.cos(lat)


def rate_of(total, depth):
    inverse = 1.0 / depth
    return DRAG * jnp.sqrt(0.125 * total * (inverse * inverse) + BACKGROUND) * inverse


def face_flow(d_re, d_im, rate, scale, omega):
    along, across = scale * rate, scale * omega
    return along * d_re + across * d_im, along * d_im - across * d_re


def unroll_of(count):
    return next((u for u in (4, 3, 5, 2) if count % u == 0), 1)


def kernel(
    sizes,
    elev, equi, depth_in, mask_in, fric_in,
    out_e, out_f,
    E, Q, E1, D, M, MI, F, AU, AV, U0, U2, V, S, FR, AX, PK, HT, PH,
    row_out, row_in, col_out, col_in, ring_out, ring_in, part_in,
    in_sem, halo_send, halo_recv, ring_send, ring_recv, part_send, part_recv, rate_send, rate_recv,
):
    rows_dev, tiles, n_cons, n_ty, n_tx = sizes
    blocks = rows_dev // 8
    last_row = PAD + rows_dev
    overlap = rows_dev - LANES
    inner_tiles, outer_tiles = tuple(range(1, tiles - 1)), (0, tiles - 1)

    c = lax.axis_index("cons")
    ty = lax.axis_index("ty")
    tx = lax.axis_index("tx")
    others = [lax.rem(c + d, n_cons) for d in range(1, n_cons)]
    owners = [lax.rem(c + n_cons - d, n_cons) for d in range(1, n_cons)]
    north, south = lax.rem(ty + 1, n_ty), lax.rem(ty + n_ty - 1, n_ty)
    east, west = lax.rem(tx + 1, n_tx), lax.rem(tx + n_tx - 1, n_tx)

    barrier = pltpu.get_barrier_semaphore()
    met = [{"cons": other} for other in others]
    met += [{"ty": north}, {"ty": south}, {"tx": east}, {"tx": west}]
    for there in met:
        pl.semaphore_signal(barrier, inc=1, device_id=there, device_id_type=MESH)

    loads = []
    for t in outer_tiles + inner_tiles:
        lanes = pl.ds(LANES * t, LANES)
        within = pl.ds(PAD, rows_dev)
        loads += [
            pltpu.make_async_copy(elev.at[:, :, :, lanes], E.at[:, :, t, within, :], in_sem.at[5 * t]),
            pltpu.make_async_copy(equi.at[:, :, :, lanes], Q.at[:, :, t, within, :], in_sem.at[5 * t + 1]),
            pltpu.make_async_copy(fric_in.at[:, lanes], F.at[t, within, :], in_sem.at[5 * t + 2]),
            pltpu.make_async_copy(depth_in.at[:, lanes], D.at[t, within, :], in_sem.at[5 * t + 3]),
            pltpu.make_async_copy(mask_in.at[:, lanes], MI.at[t], in_sem.at[5 * t + 4]),
        ]
    for load in loads:
        load.start()

    omegas = []
    for k in range(2):
        omega = jnp.float32(OMEGA_TABLE[k])
        for group in range(1, n_cons):
            omega = jnp.where(c == group, jnp.float32(OMEGA_TABLE[2 * group + k]), omega)
        omegas.append(omega)

    first_row = ty * rows_dev
    AX[...] = latitude_factor(
        first_row + lax.broadcasted_iota(jnp.int32, (rows_dev, LANES), 0), rows_dev * n_ty
    )
    ax_across = [
        latitude_factor(
            first_row + overlap * h + lax.broadcasted_iota(jnp.int32, (1, LANES), 1), rows_dev * n_ty
        )
        for h in range(2)
    ]

    lane = lax.broadcasted_iota(jnp.int32, (8, LANES), 1)
    lane_0, lane_last = lane == 0, lane == LANES - 1

    def arrive(tiles_now, copies):
        for load in copies:
            load.wait()

        @pl.loop(0, blocks, unroll=6)
        def _(b):
            for t in tiles_now:
                M[t, pl.ds(PAD + 8 * b, 8), :] = MI[t, pl.ds(8 * b, 8), :].astype(jnp.float32)

    arrive(outer_tiles, loads[:10])

    def plane_of(p, t, rows, eta, extras):
        if p < 4:
            return eta[p // 2, p % 2, t, rows, :] - Q[p // 2, p % 2, t, rows, :]
        return extras[p - 4][t, rows, :]

    def pack_columns(which, eta, extras):
        @pl.loop(0, blocks, unroll=6)
        def _(b):
            rows = pl.ds(PAD + 8 * b, 8)
            packed = jnp.zeros((8, LANES), jnp.float32)
            for p in range(4 + len(extras)):
                first = plane_of(p, 0, rows, eta, extras)
                last = plane_of(p, tiles - 1, rows, eta, extras)
                packed = jnp.where(lane == p, pltpu.roll(first, p, 1) if p else first, packed)
                packed = jnp.where(lane == 8 + p, pltpu.roll(last, 9 + p, 1), packed)
            PK[pl.ds(8 * b, 8), :] = packed

        for h in range(2):
            turned = PK[overlap * h : overlap * h + LANES, :].T
            col_out[which, 0, h] = turned[0:8]
            col_out[which, 1, h] = turned[8:16]

    def pack_rows(which, eta, extras):
        for t in range(tiles):
            for p in range(4 + len(extras)):
                row_out[which, 0, t, p : p + 1, :] = plane_of(p, t, pl.ds(PAD, 1), eta, extras)
                row_out[which, 1, t, p : p + 1, :] = plane_of(p, t, pl.ds(last_row - 1, 1), eta, extras)

    def halo_copies(which):
        copies = []
        for side, (source, target, there) in enumerate(
            (
                (col_out.at[which, 0], col_in.at[which, 1], {"tx": west}),
                (col_out.at[which, 1], col_in.at[which, 0], {"tx": east}),
                (row_out.at[which, 0], row_in.at[which, 1], {"ty": south}),
                (row_out.at[which, 1], row_in.at[which, 0], {"ty": north}),
            )
        ):
            copies.append(
                pltpu.make_async_remote_copy(
                    source, target, halo_send.at[4 * which + side], halo_recv.at[4 * which + side],
                    device_id=there, device_id_type=MESH,
                )
            )
        return copies

    groups = [(inner_tiles, a, (b - a) // 2, (b - a) // 2) for a, b in INNER] + [(inner_tiles, 0, 1, blocks - 1)]
    groups += [(outer_tiles, a, (b - a) // 2, (b - a) // 2) for a, b in OUTER]
    edges = len(INNER)

    def piece(g, owner):
        pair, first, count, step = groups[g]
        tile = pair[0] + (pair[1] - pair[0]) * (owner // 2)
        start = PAD + 8 * first + (8 * step) * lax.rem(owner, 2)
        return tile, pl.ds(pl.multiple_of(start, 8), 8 * count)

    def landing(g):
        start = 8 * sum(group[2] for group in groups[:g])
        return pl.ds(start, 8 * groups[g][2])

    def part_copy(g, d):
        tile, rows = piece(g, others[d - 1])
        return pltpu.make_async_remote_copy(
            S.at[tile, rows, :], part_in.at[d - 1, landing(g), :],
            part_send.at[g, d - 1], part_recv.at[g, d - 1],
            device_id={"cons": others[d - 1]}, device_id_type=MESH,
        )

    def rate_copy(g, d, source):
        tile, rows = piece(g, source)
        return pltpu.make_async_remote_copy(
            FR.at[tile, rows, :], FR.at[tile, rows, :],
            rate_send.at[g, d - 1], rate_recv.at[g, d - 1],
            device_id={"cons": others[d - 1]}, device_id_type=MESH,
        )

    def send_parts(g):
        for d in FAR_FIRST:
            part_copy(g, d).start()

    def settle(g):
        for d in FAR_FIRST:
            part_copy(g, d).wait_recv()
        tile, rows = piece(g, c)
        total = S[tile, rows, :]
        for d in FAR_FIRST:
            total = total + part_in[d - 1, landing(g), :]
        FR[tile, rows, :] = rate_of(total, D[tile, rows, :])
        for d in FAR_FIRST:
            rate_copy(g, d, c).start()

    def gathered(g):
        for d in FAR_FIRST:
            rate_copy(g, d, owners[d - 1]).wait_recv()

    def faces(mask, mask_next, deep, deep_next, scale):
        return -(mask * mask_next) * (0.5 * (deep + deep_next)) * scale

    def both_inverses(ru, rv, au, av, omega):
        square = omega * omega
        du, dv = ru * ru + square, rv * rv + square
        inverse = 1.0 / (du * dv)
        return au * (dv * inverse), av * (du * inverse)

    def northward(R, eta, fresh, start, which_tiles):
        rows, rows_n = pl.ds(start, 8), pl.ds(start + 1, 8)
        for t in which_tiles:
            if fresh:
                av = faces(M[t, rows, :], M[t, rows_n, :], D[t, rows, :], D[t, rows_n, :], AY_SCALE)
                AV[t, rows, :] = av
            else:
                av = AV[t, rows, :]
            rv = 0.5 * (R[t, rows, :] + R[t, rows_n, :])
            for k in range(2):
                over = av / (rv * rv + omegas[k] * omegas[k])
                d = [
                    (eta[k, p, t, rows_n, :] - Q[k, p, t, rows_n, :]) - (eta[k, p, t, rows, :] - Q[k, p, t, rows, :])
                    for p in range(2)
                ]
                v = face_flow(d[0], d[1], rv, over, omegas[k])
                for p in range(2):
                    V[k, p, t, rows, :] = v[p]

    def half_sweep(b, R, eta, fresh, inner):
        rows, rows_n, rows_s = pl.ds(PAD + 8 * b, 8), pl.ds(PAD + 8 * b + 1, 8), pl.ds(PAD + 8 * b - 1, 8)
        ax = AX[pl.ds(8 * b, 8), :]
        flowing = tuple(range(tiles - 1)) if inner else (tiles - 1,)
        closing = inner_tiles if inner else outer_tiles
        rim = None if inner else PH[pl.ds(8 * b, 8), :]

        def views(load, p):
            values = {t: load(t) for t in flowing}
            rolled = {t: pltpu.roll(values[t], LANES - 1, 1) for t in flowing}
            if inner:
                rolled[tiles - 1] = pltpu.roll(load(tiles - 1), LANES - 1, 1)
            else:
                rolled[tiles] = pltpu.roll(rim, (2 * LANES - 1 - (8 + p)) % LANES, 1)
            return values, {t: jnp.where(lane_last, rolled[t + 1], rolled[t]) for t in flowing}

        rate, rate_east = views(lambda t: R[t, rows, :], 4)
        if fresh:
            deep, deep_east = views(lambda t: D[t, rows, :], 5)
            mask, mask_east = views(lambda t: M[t, rows, :], 6)
        au, av, ru, rv = {}, {}, {}, {}
        for t in flowing:
            if fresh:
                au[t] = faces(mask[t], mask_east[t], deep[t], deep_east[t], ax)
                av[t] = faces(mask[t], M[t, rows_n, :], deep[t], D[t, rows_n, :], AY_SCALE)
                AU[t, rows, :] = au[t]
                AV[t, rows, :] = av[t]
            else:
                au[t] = AU[t, rows, :]
                av[t] = AV[t, rows, :]
            ru[t] = 0.5 * (rate[t] + rate_east[t])
            rv[t] = 0.5 * (rate[t] + R[t, rows_n, :])
        squares = {t: None for t in closing}
        theta_ax = THETA * ax
        for k in range(2):
            omega = omegas[k]
            theta_omega = THETA * omega
            zeta, zeta_east = [None, None], [None, None]
            for p in range(2):
                zeta[p], zeta_east[p] = views(lambda t: eta[k, p, t, rows, :] - Q[k, p, t, rows, :], 2 * k + p)
            flow_u, flow_v = [{}, {}], [{}, {}]
            for t in flowing:
                over_u, over_v = both_inverses(ru[t], rv[t], au[t], av[t], omega)
                u = face_flow(
                    zeta_east[0][t] - zeta[0][t], zeta_east[1][t] - zeta[1][t], ru[t], over_u, omega
                )
                north_z = [eta[k, p, t, rows_n, :] - Q[k, p, t, rows_n, :] for p in range(2)]
                v = face_flow(north_z[0] - zeta[0][t], north_z[1] - zeta[1][t], rv[t], over_v, omega)
                for p in range(2):
                    flow_u[p][t], flow_v[p][t] = u[p], v[p]
                    V[k, p, t, rows, :] = v[p]
            west_u = [{}, {}]
            for p in range(2):
                if inner:
                    rolled = {t: pltpu.roll(flow_u[p][t], 1, 1) for t in flowing}
                    U0[k, p, pl.ds(8 * b, 8), :] = flow_u[p][0]
                    U2[k, p, pl.ds(8 * b, 8), :] = rolled[tiles - 2]
                else:
                    q = 2 * k + p
                    flow_u[p][0] = U0[k, p, pl.ds(8 * b, 8), :]
                    flow_v[p][0] = V[k, p, 0, rows, :]
                    rolled = {t: pltpu.roll(flow_u[p][t], 1, 1) for t in closing}
                    rolled[-1] = pltpu.roll(rim, LANES - q, 1) if q else rim
                    rolled[tiles - 2] = U2[k, p, pl.ds(8 * b, 8), :]
                for t in closing:
                    west_u[p][t] = jnp.where(lane_0, rolled[t - 1], rolled[t])
            for t in closing:
                old = [eta[k, p, t, rows, :] for p in range(2)]
                wet = M[t, rows, :]
                for p in range(2):
                    south_v = V[k, p, t, rows_s, :]
                    turned = old[p] + theta_omega * old[1] if p == 0 else old[p] - theta_omega * old[0]
                    new = wet * (
                        turned
                        - theta_ax * (flow_u[p][t] - west_u[p][t])
                        - (THETA * AY_SCALE) * (flow_v[p][t] - south_v)
                    )
                    if fresh:
                        E1[k, p, t, rows, :] = new
                        cu = flow_u[p][t] + west_u[p][t]
                        cv = flow_v[p][t] + south_v
                        term = cu * cu + cv * cv
                        squares[t] = term if squares[t] is None else squares[t] + term
                    else:
                        out_e[k, p, pl.ds(8 * b, 8), LANES * t : LANES * (t + 1)] = new
        for t in closing:
            if fresh:
                S[t, rows, :] = squares[t]
            else:
                out_f[pl.ds(8 * b, 8), LANES * t : LANES * (t + 1)] = R[t, rows, :]

    def run(span, R, eta, fresh, inner):
        @pl.loop(span[0], span[1], unroll=unroll_of(span[1] - span[0]))
        def _(b):
            half_sweep(b, R, eta, fresh, inner)

    pack_columns(0, E, (F, D, M))
    arrive(inner_tiles, loads[10:])
    pack_rows(0, E, (F, D, M))
    pl.semaphore_wait(barrier, len(met))
    halo_one = halo_copies(0)
    for copy in halo_one:
        copy.start()
    northward(F, E, True, PAD, inner_tiles)
    for g in (0, 1):
        run(INNER[g], F, E, True, True)
        send_parts(g)
    for copy in halo_one:
        copy.wait_recv()

    inside_north = jnp.where(ty == n_ty - 1, jnp.float32(0), jnp.float32(1))
    inside_south = jnp.where(ty == 0, jnp.float32(0), jnp.float32(1))
    for t in range(tiles):
        for side, row, keep in ((0, PAD - 1, inside_south), (1, last_row, inside_north)):
            line = pl.ds(row, 1)
            for p in range(4):
                E[p // 2, p % 2, t, line, :] = row_in[0, side, t, p : p + 1, :]
                Q[p // 2, p % 2, t, line, :] = jnp.zeros((1, LANES), jnp.float32)
            F[t, line, :] = row_in[0, side, t, 4:5, :]
            D[t, line, :] = row_in[0, side, t, 5:6, :]
            M[t, line, :] = row_in[0, side, t, 6:7, :] * keep

    def western_flow(h, which, rate):
        own, other = col_out.at[which, 0, h], col_in.at[which, 0, h]
        here, there = col_out.at[0, 0, h], col_in.at[0, 0, h]
        scale = faces(here[6:7, :], there[6:7, :], here[5:6, :], there[5:6, :], ax_across[h])
        for k in range(2):
            over = scale / (rate * rate + omegas[k] * omegas[k])
            d_re = own[2 * k : 2 * k + 1, :] - other[2 * k : 2 * k + 1, :]
            d_im = own[2 * k + 1 : 2 * k + 2, :] - other[2 * k + 1 : 2 * k + 2, :]
            u_re, u_im = face_flow(d_re, d_im, rate, over, omegas[k])
            HT[h, 2 * k : 2 * k + 1, :] = u_re
            HT[h, 2 * k + 1 : 2 * k + 2, :] = u_im

    def turn_back():
        PH[0:LANES, :] = HT[0].T
        PH[LANES:rows_dev, :] = HT[1].T[LANES - overlap :]

    for h in range(2):
        HT[h] = jnp.zeros((LANES, LANES), jnp.float32)
        HT[h, 8:16, :] = col_in[0, 1, h]
        western_flow(h, 0, 0.5 * (col_out[0, 0, h, 4:5, :] + col_in[0, 0, h, 4:5, :]))
    turn_back()
    northward(F, E, True, 0, range(tiles))
    for b in (0, blocks - 1):
        half_sweep(b, F, E, True, True)
    send_parts(edges)
    first_outer = edges + 1
    for i, span in enumerate(OUTER):
        run(span, F, E, True, False)
        send_parts(first_outer + i)

    pack_columns(1, E1, (S,))
    pack_rows(1, E1, (S,))
    halo_two = halo_copies(1)
    for copy in halo_two:
        copy.start()
    for g in range(first_outer):
        settle(g)
    settle(first_outer)
    for copy in halo_two:
        copy.wait_recv()
    for t in range(tiles):
        ring_out[t : t + 1, :] = row_in[1, 0, t, 4:5, :]
        ring_out[tiles + t : tiles + t + 1, :] = row_in[1, 1, t, 4:5, :]
    for h in range(2):
        ring_out[8 + h : 9 + h, :] = col_in[1, 0, h, 4:5, :]
        ring_out[10 + h : 11 + h, :] = col_in[1, 1, h, 4:5, :]
        ring_out[12 + h : 13 + h, :] = col_out[1, 0, h, 4:5, :]
    ring_out[14:16, :] = jnp.zeros((2, LANES), jnp.float32)
    ring = [
        pltpu.make_async_remote_copy(
            ring_out, ring_in.at[d - 1], ring_send.at[d - 1], ring_recv.at[d - 1],
            device_id={"cons": others[d - 1]}, device_id_type=MESH,
        )
        for d in range(1, n_cons)
    ]
    for copy in ring:
        copy.start()
    for g in range(first_outer + 1, len(groups)):
        settle(g)

    for g in (0, edges, first_outer):
        gathered(g)
    northward(FR, E1, False, PAD, inner_tiles)
    gathered(1)
    run((1, 11), FR, E1, False, True)

    for copy in ring:
        copy.wait_recv()

    def ring_rate(line, depth):
        rows = slice(line, line + 1)
        total = (ring_out[rows, :] + ring_in[0, rows, :]) + (ring_in[1, rows, :] + ring_in[2, rows, :])
        return rate_of(total, depth)

    for t in range(tiles):
        for side, row in ((0, PAD - 1), (1, last_row)):
            line = pl.ds(row, 1)
            for p in range(4):
                E1[p // 2, p % 2, t, line, :] = row_in[1, side, t, p : p + 1, :]
            FR[t, line, :] = ring_rate(tiles * side + t, row_in[0, side, t, 5:6, :])
    for h in range(2):
        rate_west = ring_rate(8 + h, col_in[0, 0, h, 5:6, :])
        rate_east = ring_rate(10 + h, col_in[0, 1, h, 5:6, :])
        rate_own = ring_rate(12 + h, col_out[0, 0, h, 5:6, :])
        HT[h, 8:12, :] = col_in[1, 1, h, 0:4, :]
        HT[h, 12:13, :] = rate_east
        western_flow(h, 1, 0.5 * (rate_own + rate_west))
    turn_back()
    northward(FR, E1, False, 0, range(tiles))
    half_sweep(0, FR, E1, False, True)
    run((0, 3), FR, E1, False, False)
    run((3, 11), FR, E1, False, False)
    gathered(first_outer + 1)
    run((11, 17), FR, E1, False, True)
    half_sweep(blocks - 1, FR, E1, False, True)
    run((11, 15), FR, E1, False, False)
    run((15, blocks), FR, E1, False, False)

    for copy in halo_one + halo_two + ring:
        copy.wait_send()
    for g in range(len(groups)):
        for d in FAR_FIRST:
            part_copy(g, d).wait_send()
            rate_copy(g, d, c).wait_send()


def solution(mesh):
    n_cons, n_ty, n_tx = (mesh.shape[axis] for axis in ("cons", "ty", "tx"))

    def body(elevation, equilibrium, depth, land_mask, friction_prev):
        kdev, two, rows_dev, cols_dev = elevation.shape
        tiles = cols_dev // LANES
        tall = rows_dev + 2 * PAD
        f32 = jnp.float32
        field = pltpu.VMEM((tiles, tall, LANES), f32)
        fields = pltpu.VMEM((2, 2, tiles, tall, LANES), f32)
        n_groups = len(INNER) + len(OUTER) + 1
        hbm = pl.BlockSpec(memory_space=pltpu.HBM)
        vmem = pl.BlockSpec(memory_space=pltpu.VMEM)
        return pl.pallas_call(
            functools.partial(kernel, (rows_dev, tiles, n_cons, n_ty, n_tx)),
            out_shape=(
                pltpu.VMEM(elevation.shape, f32),
                pltpu.VMEM(depth.shape, f32),
            ),
            in_specs=[hbm] * 5,
            out_specs=(vmem, vmem),
            scratch_shapes=[
                fields, fields, fields, field, field,
                pltpu.VMEM((tiles, rows_dev, LANES), jnp.int32),
                field, field, field,
                pltpu.VMEM((2, 2, rows_dev, LANES), f32),
                pltpu.VMEM((2, 2, rows_dev, LANES), f32),
                fields, field, field,
                pltpu.VMEM((rows_dev, LANES), f32),
                pltpu.VMEM((rows_dev, LANES), f32),
                pltpu.VMEM((2, LANES, LANES), f32),
                pltpu.VMEM((rows_dev, LANES), f32),
                pltpu.VMEM((2, 2, tiles, 8, LANES), f32),
                pltpu.VMEM((2, 2, tiles, 8, LANES), f32),
                pltpu.VMEM((2, 2, 2, 8, LANES), f32),
                pltpu.VMEM((2, 2, 2, 8, LANES), f32),
                pltpu.VMEM((16, LANES), f32),
                pltpu.VMEM((n_cons - 1, 16, LANES), f32),
                pltpu.VMEM((n_cons - 1, rows_dev, LANES), f32),
                pltpu.SemaphoreType.DMA((5 * tiles,)),
                pltpu.SemaphoreType.DMA((8,)),
                pltpu.SemaphoreType.DMA((8,)),
                pltpu.SemaphoreType.DMA((n_cons - 1,)),
                pltpu.SemaphoreType.DMA((n_cons - 1,)),
                pltpu.SemaphoreType.DMA((n_groups, n_cons - 1)),
                pltpu.SemaphoreType.DMA((n_groups, n_cons - 1)),
                pltpu.SemaphoreType.DMA((n_groups, n_cons - 1)),
                pltpu.SemaphoreType.DMA((n_groups, n_cons - 1)),
            ],
            compiler_params=pltpu.CompilerParams(collective_id=0, has_side_effects=True, vmem_limit_bytes=56 * 2**20),
        )(elevation, equilibrium, depth, land_mask, friction_prev)

    tiled = P("ty", "tx")
    planes = P("cons", None, "ty", "tx")
    return jax.shard_map(
        body,
        mesh=mesh,
        in_specs=(planes, planes, tiled, tiled, tiled),
        out_specs=(planes, tiled),
        check_vma=False,
    )
```

```python
import functools
import math

import jax
import jax.numpy as jnp
from jax import lax
from jax.experimental import pallas as pl
from jax.experimental.pallas import tpu as pltpu
from jax.sharding import PartitionSpec as P

OMEGA_TABLE = (1.0, 1.0351, 0.9582, 1.0379, 0.5181, 0.4816, 0.5164, 0.4454)
AY_SCALE = 0.5
THETA = 0.05
DRAG = 0.5
BACKGROUND = 0.01

MESH = pl.DeviceIdType.MESH
LANES = 128
PAD = 8
FAR_FIRST = (2, 1, 3)
INNER = ((1, 9), (9, 17))
OUTER = ((0, 12), (12, 18))


def latitude_factor(rows, total):
    lat = (-60.0 + 120.0 * (rows.astype(jnp.float32) + 0.5) / total) * (math.pi / 180.0)
    return 0.5 / jnp.cos(lat)


def rate_of(total, depth):
    inverse = 1.0 / depth
    return DRAG * jnp.sqrt(0.125 * total * (inverse * inverse) + BACKGROUND) * inverse


def face_flow(d_re, d_im, rate, scale, omega):
    along, across = scale * rate, scale * omega
    return along * d_re + across * d_im, along * d_im - across * d_re


def unroll_of(count):
    return next((u for u in (4, 3, 5, 2) if count % u == 0), 1)


def kernel(
    sizes,
    elev, equi, depth_in, mask_in, fric_in,
    out_e, out_f,
    E, Q, E1, D, M, MI, F, AU, AV, U0, U2, V, S, FR, AX, PK, HT, PH,
    row_out, row_in, col_out, col_in, ring_out, ring_in, part_in,
    in_sem, halo_send, halo_recv, ring_send, ring_recv, part_send, part_recv, rate_send, rate_recv,
):
    rows_dev, tiles, n_cons, n_ty, n_tx = sizes
    blocks = rows_dev // 8
    last_row = PAD + rows_dev
    overlap = rows_dev - LANES
    inner_tiles, outer_tiles = tuple(range(1, tiles - 1)), (0, tiles - 1)

    c = lax.axis_index("cons")
    ty = lax.axis_index("ty")
    tx = lax.axis_index("tx")
    others = [lax.rem(c + d, n_cons) for d in range(1, n_cons)]
    owners = [lax.rem(c + n_cons - d, n_cons) for d in range(1, n_cons)]
    north, south = lax.rem(ty + 1, n_ty), lax.rem(ty + n_ty - 1, n_ty)
    east, west = lax.rem(tx + 1, n_tx), lax.rem(tx + n_tx - 1, n_tx)

    barrier = pltpu.get_barrier_semaphore()
    met = [{"cons": other} for other in others]
    met += [{"ty": north}, {"ty": south}, {"tx": east}, {"tx": west}]
    for there in met:
        pl.semaphore_signal(barrier, inc=1, device_id=there, device_id_type=MESH)

    loads = []
    for t in outer_tiles + inner_tiles:
        lanes = pl.ds(LANES * t, LANES)
        within = pl.ds(PAD, rows_dev)
        loads += [
            pltpu.make_async_copy(elev.at[:, :, :, lanes], E.at[:, :, t, within, :], in_sem.at[5 * t]),
            pltpu.make_async_copy(equi.at[:, :, :, lanes], Q.at[:, :, t, within, :], in_sem.at[5 * t + 1]),
            pltpu.make_async_copy(fric_in.at[:, lanes], F.at[t, within, :], in_sem.at[5 * t + 2]),
            pltpu.make_async_copy(depth_in.at[:, lanes], D.at[t, within, :], in_sem.at[5 * t + 3]),
            pltpu.make_async_copy(mask_in.at[:, lanes], MI.at[t], in_sem.at[5 * t + 4]),
        ]
    for load in loads:
        load.start()

    omegas = []
    for k in range(2):
        omega = jnp.float32(OMEGA_TABLE[k])
        for group in range(1, n_cons):
            omega = jnp.where(c == group, jnp.float32(OMEGA_TABLE[2 * group + k]), omega)
        omegas.append(omega)

    first_row = ty * rows_dev
    AX[...] = latitude_factor(
        first_row + lax.broadcasted_iota(jnp.int32, (rows_dev, LANES), 0), rows_dev * n_ty
    )
    ax_across = [
        latitude_factor(
            first_row + overlap * h + lax.broadcasted_iota(jnp.int32, (1, LANES), 1), rows_dev * n_ty
        )
        for h in range(2)
    ]

    lane = lax.broadcasted_iota(jnp.int32, (8, LANES), 1)
    lane_0, lane_last = lane == 0, lane == LANES - 1

    def arrive(tiles_now, copies):
        for load in copies:
            load.wait()

        @pl.loop(0, blocks, unroll=6)
        def _(b):
            for t in tiles_now:
                M[t, pl.ds(PAD + 8 * b, 8), :] = MI[t, pl.ds(8 * b, 8), :].astype(jnp.float32)

    arrive(outer_tiles, loads[:10])

    def plane_of(p, t, rows, eta, extras):
        if p < 4:
            return eta[p // 2, p % 2, t, rows, :] - Q[p // 2, p % 2, t, rows, :]
        return extras[p - 4][t, rows, :]

    def pack_columns(which, eta, extras):
        @pl.loop(0, blocks, unroll=6)
        def _(b):
            rows = pl.ds(PAD + 8 * b, 8)
            packed = jnp.zeros((8, LANES), jnp.float32)
            for p in range(4 + len(extras)):
                first = plane_of(p, 0, rows, eta, extras)
                last = plane_of(p, tiles - 1, rows, eta, extras)
                packed = jnp.where(lane == p, pltpu.roll(first, p, 1) if p else first, packed)
                packed = jnp.where(lane == 8 + p, pltpu.roll(last, 9 + p, 1), packed)
            PK[pl.ds(8 * b, 8), :] = packed

        for h in range(2):
            turned = PK[overlap * h : overlap * h + LANES, :].T
            col_out[which, 0, h] = turned[0:8]
            col_out[which, 1, h] = turned[8:16]

    def pack_rows(which, eta, extras):
        for t in range(tiles):
            for p in range(4 + len(extras)):
                row_out[which, 0, t, p : p + 1, :] = plane_of(p, t, pl.ds(PAD, 1), eta, extras)
                row_out[which, 1, t, p : p + 1, :] = plane_of(p, t, pl.ds(last_row - 1, 1), eta, extras)

    def halo_copies(which):
        copies = []
        for side, (source, target, there) in enumerate(
            (
                (col_out.at[which, 0], col_in.at[which, 1], {"tx": west}),
                (col_out.at[which, 1], col_in.at[which, 0], {"tx": east}),
                (row_out.at[which, 0], row_in.at[which, 1], {"ty": south}),
                (row_out.at[which, 1], row_in.at[which, 0], {"ty": north}),
            )
        ):
            copies.append(
                pltpu.make_async_remote_copy(
                    source, target, halo_send.at[4 * which + side], halo_recv.at[4 * which + side],
                    device_id=there, device_id_type=MESH,
                )
            )
        return copies

    groups = [(inner_tiles, a, (b - a) // 2, (b - a) // 2) for a, b in INNER] + [(inner_tiles, 0, 1, blocks - 1)]
    groups += [(outer_tiles, a, (b - a) // 2, (b - a) // 2) for a, b in OUTER]
    edges = len(INNER)

    def piece(g, owner):
        pair, first, count, step = groups[g]
        tile = pair[0] + (pair[1] - pair[0]) * (owner // 2)
        start = PAD + 8 * first + (8 * step) * lax.rem(owner, 2)
        return tile, pl.ds(pl.multiple_of(start, 8), 8 * count)

    def landing(g):
        start = 8 * sum(group[2] for group in groups[:g])
        return pl.ds(start, 8 * groups[g][2])

    def part_copy(g, d):
        tile, rows = piece(g, others[d - 1])
        return pltpu.make_async_remote_copy(
            S.at[tile, rows, :], part_in.at[d - 1, landing(g), :],
            part_send.at[g, d - 1], part_recv.at[g, d - 1],
            device_id={"cons": others[d - 1]}, device_id_type=MESH,
        )

    def rate_copy(g, d, source):
        tile, rows = piece(g, source)
        return pltpu.make_async_remote_copy(
            FR.at[tile, rows, :], FR.at[tile, rows, :],
            rate_send.at[g, d - 1], rate_recv.at[g, d - 1],
            device_id={"cons": others[d - 1]}, device_id_type=MESH,
        )

    def send_parts(g):
        for d in FAR_FIRST:
            part_copy(g, d).start()

    def settle(g):
        for d in FAR_FIRST:
            part_copy(g, d).wait_recv()
        tile, rows = piece(g, c)
        total = S[tile, rows, :]
        for d in FAR_FIRST:
            total = total + part_in[d - 1, landing(g), :]
        FR[tile, rows, :] = rate_of(total, D[tile, rows, :])
        for d in FAR_FIRST:
            rate_copy(g, d, c).start()

    def gathered(g):
        for d in FAR_FIRST:
            rate_copy(g, d, owners[d - 1]).wait_recv()

    def faces(mask, mask_next, deep, deep_next, scale):
        return -(mask * mask_next) * (0.5 * (deep + deep_next)) * scale

    def both_inverses(ru, rv, au, av, omega):
        square = omega * omega
        du, dv = ru * ru + square, rv * rv + square
        inverse = 1.0 / (du * dv)
        return au * (dv * inverse), av * (du * inverse)

    def northward(R, eta, fresh, start, which_tiles):
        rows, rows_n = pl.ds(start, 8), pl.ds(start + 1, 8)
        for t in which_tiles:
            if fresh:
                av = faces(M[t, rows, :], M[t, rows_n, :], D[t, rows, :], D[t, rows_n, :], AY_SCALE)
                AV[t, rows, :] = av
            else:
                av = AV[t, rows, :]
            rv = 0.5 * (R[t, rows, :] + R[t, rows_n, :])
            for k in range(2):
                over = av / (rv * rv + omegas[k] * omegas[k])
                d = [
                    (eta[k, p, t, rows_n, :] - Q[k, p, t, rows_n, :]) - (eta[k, p, t, rows, :] - Q[k, p, t, rows, :])
                    for p in range(2)
                ]
                v = face_flow(d[0], d[1], rv, over, omegas[k])
                for p in range(2):
                    V[k, p, t, rows, :] = v[p]

    def half_sweep(b, R, eta, fresh, inner):
        rows, rows_n, rows_s = pl.ds(PAD + 8 * b, 8), pl.ds(PAD + 8 * b + 1, 8), pl.ds(PAD + 8 * b - 1, 8)
        ax = AX[pl.ds(8 * b, 8), :]
        flowing = tuple(range(tiles - 1)) if inner else (tiles - 1,)
        closing = inner_tiles if inner else outer_tiles
        rim = None if inner else PH[pl.ds(8 * b, 8), :]

        def views(load, p):
            values = {t: load(t) for t in flowing}
            rolled = {t: pltpu.roll(values[t], LANES - 1, 1) for t in flowing}
            if inner:
                rolled[tiles - 1] = pltpu.roll(load(tiles - 1), LANES - 1, 1)
            else:
                rolled[tiles] = pltpu.roll(rim, (2 * LANES - 1 - (8 + p)) % LANES, 1)
            return values, {t: jnp.where(lane_last, rolled[t + 1], rolled[t]) for t in flowing}

        rate, rate_east = views(lambda t: R[t, rows, :], 4)
        if fresh:
            deep, deep_east = views(lambda t: D[t, rows, :], 5)
            mask, mask_east = views(lambda t: M[t, rows, :], 6)
        au, av, ru, rv = {}, {}, {}, {}
        for t in flowing:
            if fresh:
                au[t] = faces(mask[t], mask_east[t], deep[t], deep_east[t], ax)
                av[t] = faces(mask[t], M[t, rows_n, :], deep[t], D[t, rows_n, :], AY_SCALE)
                AU[t, rows, :] = au[t]
                AV[t, rows, :] = av[t]
            else:
                au[t] = AU[t, rows, :]
                av[t] = AV[t, rows, :]
            ru[t] = 0.5 * (rate[t] + rate_east[t])
            rv[t] = 0.5 * (rate[t] + R[t, rows_n, :])
        squares = {t: None for t in closing}
        theta_ax = THETA * ax
        for k in range(2):
            omega = omegas[k]
            theta_omega = THETA * omega
            zeta, zeta_east = [None, None], [None, None]
            for p in range(2):
                zeta[p], zeta_east[p] = views(lambda t: eta[k, p, t, rows, :] - Q[k, p, t, rows, :], 2 * k + p)
            flow_u, flow_v = [{}, {}], [{}, {}]
            for t in flowing:
                over_u, over_v = both_inverses(ru[t], rv[t], au[t], av[t], omega)
                u = face_flow(
                    zeta_east[0][t] - zeta[0][t], zeta_east[1][t] - zeta[1][t], ru[t], over_u, omega
                )
                north_z = [eta[k, p, t, rows_n, :] - Q[k, p, t, rows_n, :] for p in range(2)]
                v = face_flow(north_z[0] - zeta[0][t], north_z[1] - zeta[1][t], rv[t], over_v, omega)
                for p in range(2):
                    flow_u[p][t], flow_v[p][t] = u[p], v[p]
                    V[k, p, t, rows, :] = v[p]
            west_u = [{}, {}]
            for p in range(2):
                if inner:
                    rolled = {t: pltpu.roll(flow_u[p][t], 1, 1) for t in flowing}
                    U0[k, p, pl.ds(8 * b, 8), :] = flow_u[p][0]
                    U2[k, p, pl.ds(8 * b, 8), :] = rolled[tiles - 2]
                else:
                    q = 2 * k + p
                    flow_u[p][0] = U0[k, p, pl.ds(8 * b, 8), :]
                    flow_v[p][0] = V[k, p, 0, rows, :]
                    rolled = {t: pltpu.roll(flow_u[p][t], 1, 1) for t in closing}
                    rolled[-1] = pltpu.roll(rim, LANES - q, 1) if q else rim
                    rolled[tiles - 2] = U2[k, p, pl.ds(8 * b, 8), :]
                for t in closing:
                    west_u[p][t] = jnp.where(lane_0, rolled[t - 1], rolled[t])
            for t in closing:
                old = [eta[k, p, t, rows, :] for p in range(2)]
                wet = M[t, rows, :]
                for p in range(2):
                    south_v = V[k, p, t, rows_s, :]
                    turned = old[p] + theta_omega * old[1] if p == 0 else old[p] - theta_omega * old[0]
                    new = wet * (
                        turned
                        - theta_ax * (flow_u[p][t] - west_u[p][t])
                        - (THETA * AY_SCALE) * (flow_v[p][t] - south_v)
                    )
                    if fresh:
                        E1[k, p, t, rows, :] = new
                        cu = flow_u[p][t] + west_u[p][t]
                        cv = flow_v[p][t] + south_v
                        term = cu * cu + cv * cv
                        squares[t] = term if squares[t] is None else squares[t] + term
                    else:
                        out_e[k, p, pl.ds(8 * b, 8), LANES * t : LANES * (t + 1)] = new
        for t in closing:
            if fresh:
                S[t, rows, :] = squares[t]
            else:
                out_f[pl.ds(8 * b, 8), LANES * t : LANES * (t + 1)] = R[t, rows, :]

    def run(span, R, eta, fresh, inner):
        @pl.loop(span[0], span[1], unroll=unroll_of(span[1] - span[0]))
        def _(b):
            half_sweep(b, R, eta, fresh, inner)

    pack_columns(0, E, (F, D, M))
    arrive(inner_tiles, loads[10:])
    pack_rows(0, E, (F, D, M))
    pl.semaphore_wait(barrier, len(met))
    halo_one = halo_copies(0)
    for copy in halo_one:
        copy.start()
    northward(F, E, True, PAD, inner_tiles)
    for g in (0, 1):
        run(INNER[g], F, E, True, True)
        send_parts(g)
    for copy in halo_one[:2]:
        copy.wait_recv()

    def western_flow(h, which, rate):
        own, other = col_out.at[which, 0, h], col_in.at[which, 0, h]
        here, there = col_out.at[0, 0, h], col_in.at[0, 0, h]
        scale = faces(here[6:7, :], there[6:7, :], here[5:6, :], there[5:6, :], ax_across[h])
        for k in range(2):
            over = scale / (rate * rate + omegas[k] * omegas[k])
            d_re = own[2 * k : 2 * k + 1, :] - other[2 * k : 2 * k + 1, :]
            d_im = own[2 * k + 1 : 2 * k + 2, :] - other[2 * k + 1 : 2 * k + 2, :]
            u_re, u_im = face_flow(d_re, d_im, rate, over, omegas[k])
            HT[h, 2 * k : 2 * k + 1, :] = u_re
            HT[h, 2 * k + 1 : 2 * k + 2, :] = u_im

    def turn_back():
        PH[0:LANES, :] = HT[0].T
        PH[LANES:rows_dev, :] = HT[1].T[LANES - overlap :]

    for h in range(2):
        HT[h] = jnp.zeros((LANES, LANES), jnp.float32)
        HT[h, 8:16, :] = col_in[0, 1, h]
        western_flow(h, 0, 0.5 * (col_out[0, 0, h, 4:5, :] + col_in[0, 0, h, 4:5, :]))
    turn_back()
    for copy in halo_one[2:]:
        copy.wait_recv()

    inside_north = jnp.where(ty == n_ty - 1, jnp.float32(0), jnp.float32(1))
    inside_south = jnp.where(ty == 0, jnp.float32(0), jnp.float32(1))
    for t in range(tiles):
        for side, row, keep in ((0, PAD - 1, inside_south), (1, last_row, inside_north)):
            line = pl.ds(row, 1)
            for p in range(4):
                E[p // 2, p % 2, t, line, :] = row_in[0, side, t, p : p + 1, :]
                Q[p // 2, p % 2, t, line, :] = jnp.zeros((1, LANES), jnp.float32)
            F[t, line, :] = row_in[0, side, t, 4:5, :]
            D[t, line, :] = row_in[0, side, t, 5:6, :]
            M[t, line, :] = row_in[0, side, t, 6:7, :] * keep
    northward(F, E, True, 0, range(tiles))
    for b in (0, blocks - 1):
        half_sweep(b, F, E, True, True)
    send_parts(edges)
    first_outer = edges + 1
    for i, span in enumerate(OUTER):
        run(span, F, E, True, False)
        send_parts(first_outer + i)

    halo_two = halo_copies(1)
    pack_rows(1, E1, (S,))
    for copy in halo_two[2:]:
        copy.start()
    pack_columns(1, E1, (S,))
    for copy in halo_two[:2]:
        copy.start()
    for g in range(first_outer):
        settle(g)
    settle(first_outer)
    for copy in halo_two:
        copy.wait_recv()
    for t in range(tiles):
        ring_out[t : t + 1, :] = row_in[1, 0, t, 4:5, :]
        ring_out[tiles + t : tiles + t + 1, :] = row_in[1, 1, t, 4:5, :]
    for h in range(2):
        ring_out[8 + h : 9 + h, :] = col_in[1, 0, h, 4:5, :]
        ring_out[10 + h : 11 + h, :] = col_in[1, 1, h, 4:5, :]
        ring_out[12 + h : 13 + h, :] = col_out[1, 0, h, 4:5, :]
    ring_out[14:16, :] = jnp.zeros((2, LANES), jnp.float32)
    ring = [
        pltpu.make_async_remote_copy(
            ring_out, ring_in.at[d - 1], ring_send.at[d - 1], ring_recv.at[d - 1],
            device_id={"cons": others[d - 1]}, device_id_type=MESH,
        )
        for d in range(1, n_cons)
    ]
    for copy in ring:
        copy.start()
    for g in range(first_outer + 1, len(groups)):
        settle(g)

    for g in (0, edges, first_outer):
        gathered(g)
    northward(FR, E1, False, PAD, inner_tiles)
    gathered(1)
    run((1, 11), FR, E1, False, True)

    for copy in ring:
        copy.wait_recv()

    def ring_rate(line, depth):
        rows = slice(line, line + 1)
        total = (ring_out[rows, :] + ring_in[0, rows, :]) + (ring_in[1, rows, :] + ring_in[2, rows, :])
        return rate_of(total, depth)

    for t in range(tiles):
        for side, row in ((0, PAD - 1), (1, last_row)):
            line = pl.ds(row, 1)
            for p in range(4):
                E1[p // 2, p % 2, t, line, :] = row_in[1, side, t, p : p + 1, :]
            FR[t, line, :] = ring_rate(tiles * side + t, row_in[0, side, t, 5:6, :])
    for h in range(2):
        rate_west = ring_rate(8 + h, col_in[0, 0, h, 5:6, :])
        rate_east = ring_rate(10 + h, col_in[0, 1, h, 5:6, :])
        rate_own = ring_rate(12 + h, col_out[0, 0, h, 5:6, :])
        HT[h, 8:12, :] = col_in[1, 1, h, 0:4, :]
        HT[h, 12:13, :] = rate_east
        western_flow(h, 1, 0.5 * (rate_own + rate_west))
    turn_back()
    northward(FR, E1, False, 0, range(tiles))
    half_sweep(0, FR, E1, False, True)
    run((0, 3), FR, E1, False, False)
    run((3, 11), FR, E1, False, False)
    gathered(first_outer + 1)
    run((11, 17), FR, E1, False, True)
    half_sweep(blocks - 1, FR, E1, False, True)
    run((11, 15), FR, E1, False, False)
    run((15, blocks), FR, E1, False, False)

    for copy in halo_one + halo_two + ring:
        copy.wait_send()
    for g in range(len(groups)):
        for d in FAR_FIRST:
            part_copy(g, d).wait_send()
            rate_copy(g, d, c).wait_send()


def solution(mesh):
    n_cons, n_ty, n_tx = (mesh.shape[axis] for axis in ("cons", "ty", "tx"))

    def body(elevation, equilibrium, depth, land_mask, friction_prev):
        kdev, two, rows_dev, cols_dev = elevation.shape
        tiles = cols_dev // LANES
        tall = rows_dev + 2 * PAD
        f32 = jnp.float32
        field = pltpu.VMEM((tiles, tall, LANES), f32)
        fields = pltpu.VMEM((2, 2, tiles, tall, LANES), f32)
        n_groups = len(INNER) + len(OUTER) + 1
        hbm = pl.BlockSpec(memory_space=pltpu.HBM)
        vmem = pl.BlockSpec(memory_space=pltpu.VMEM)
        return pl.pallas_call(
            functools.partial(kernel, (rows_dev, tiles, n_cons, n_ty, n_tx)),
            out_shape=(
                pltpu.VMEM(elevation.shape, f32),
                pltpu.VMEM(depth.shape, f32),
            ),
            in_specs=[hbm] * 5,
            out_specs=(vmem, vmem),
            scratch_shapes=[
                fields, fields, fields, field, field,
                pltpu.VMEM((tiles, rows_dev, LANES), jnp.int32),
                field, field, field,
                pltpu.VMEM((2, 2, rows_dev, LANES), f32),
                pltpu.VMEM((2, 2, rows_dev, LANES), f32),
                fields, field, field,
                pltpu.VMEM((rows_dev, LANES), f32),
                pltpu.VMEM((rows_dev, LANES), f32),
                pltpu.VMEM((2, LANES, LANES), f32),
                pltpu.VMEM((rows_dev, LANES), f32),
                pltpu.VMEM((2, 2, tiles, 8, LANES), f32),
                pltpu.VMEM((2, 2, tiles, 8, LANES), f32),
                pltpu.VMEM((2, 2, 2, 8, LANES), f32),
                pltpu.VMEM((2, 2, 2, 8, LANES), f32),
                pltpu.VMEM((16, LANES), f32),
                pltpu.VMEM((n_cons - 1, 16, LANES), f32),
                pltpu.VMEM((n_cons - 1, rows_dev, LANES), f32),
                pltpu.SemaphoreType.DMA((5 * tiles,)),
                pltpu.SemaphoreType.DMA((8,)),
                pltpu.SemaphoreType.DMA((8,)),
                pltpu.SemaphoreType.DMA((n_cons - 1,)),
                pltpu.SemaphoreType.DMA((n_cons - 1,)),
                pltpu.SemaphoreType.DMA((n_groups, n_cons - 1)),
                pltpu.SemaphoreType.DMA((n_groups, n_cons - 1)),
                pltpu.SemaphoreType.DMA((n_groups, n_cons - 1)),
                pltpu.SemaphoreType.DMA((n_groups, n_cons - 1)),
            ],
            compiler_params=pltpu.CompilerParams(collective_id=0, has_side_effects=True, vmem_limit_bytes=56 * 2**20),
        )(elevation, equilibrium, depth, land_mask, friction_prev)

    tiled = P("ty", "tx")
    planes = P("cons", None, "ty", "tx")
    return jax.shard_map(
        body,
        mesh=mesh,
        in_specs=(planes, planes, tiled, tiled, tiled),
        out_specs=(planes, tiled),
        check_vma=False,
    )
```

```python
import functools
import math

import jax
import jax.numpy as jnp
from jax import lax
from jax.experimental import pallas as pl
from jax.experimental.pallas import tpu as pltpu
from jax.sharding import PartitionSpec as P

OMEGA_TABLE = (1.0, 1.0351, 0.9582, 1.0379, 0.5181, 0.4816, 0.5164, 0.4454)
AY_SCALE = 0.5
THETA = 0.05
DRAG = 0.5
BACKGROUND = 0.01

MESH = pl.DeviceIdType.MESH
LANES = 128
PAD = 8
FAR_FIRST = (2, 1, 3)
INNER = ((1, 9), (9, 17))
OUTER = ((0, 12), (12, 18))


def latitude_factor(rows, total):
    lat = (-60.0 + 120.0 * (rows.astype(jnp.float32) + 0.5) / total) * (math.pi / 180.0)
    return 0.5 / jnp.cos(lat)


def rate_of(total, depth):
    inverse = 1.0 / depth
    return DRAG * jnp.sqrt(0.125 * total * (inverse * inverse) + BACKGROUND) * inverse


def face_flow(d_re, d_im, rate, scale, omega):
    along, across = scale * rate, scale * omega
    return along * d_re + across * d_im, along * d_im - across * d_re


def unroll_of(count):
    return next((u for u in (4, 3, 5, 2) if count % u == 0), 1)


def kernel(
    sizes,
    elev, equi, depth_in, mask_in, fric_in,
    out_e, out_f,
    E, Q, E1, D, M, MI, F, AU, AV, U0, U2, V, S, FR, AX, PK, HT, PH,
    row_out, row_in, col_out, col_in, ring_out, ring_in, part_in,
    in_sem, halo_send, halo_recv, ring_send, ring_recv, part_send, part_recv, rate_send, rate_recv,
):
    rows_dev, tiles, n_cons, n_ty, n_tx = sizes
    blocks = rows_dev // 8
    last_row = PAD + rows_dev
    overlap = rows_dev - LANES
    inner_tiles, outer_tiles = tuple(range(1, tiles - 1)), (0, tiles - 1)

    c = lax.axis_index("cons")
    ty = lax.axis_index("ty")
    tx = lax.axis_index("tx")
    others = [lax.rem(c + d, n_cons) for d in range(1, n_cons)]
    owners = [lax.rem(c + n_cons - d, n_cons) for d in range(1, n_cons)]
    north, south = lax.rem(ty + 1, n_ty), lax.rem(ty + n_ty - 1, n_ty)
    east, west = lax.rem(tx + 1, n_tx), lax.rem(tx + n_tx - 1, n_tx)

    barrier = pltpu.get_barrier_semaphore()
    met = [{"cons": other} for other in others]
    met += [{"ty": north}, {"ty": south}, {"tx": east}, {"tx": west}]
    for there in met:
        pl.semaphore_signal(barrier, inc=1, device_id=there, device_id_type=MESH)

    loads = []
    for t in outer_tiles + inner_tiles:
        lanes = pl.ds(LANES * t, LANES)
        within = pl.ds(PAD, rows_dev)
        loads += [
            pltpu.make_async_copy(elev.at[:, :, :, lanes], E.at[:, :, t, within, :], in_sem.at[5 * t]),
            pltpu.make_async_copy(equi.at[:, :, :, lanes], Q.at[:, :, t, within, :], in_sem.at[5 * t + 1]),
            pltpu.make_async_copy(fric_in.at[:, lanes], F.at[t, within, :], in_sem.at[5 * t + 2]),
            pltpu.make_async_copy(depth_in.at[:, lanes], D.at[t, within, :], in_sem.at[5 * t + 3]),
            pltpu.make_async_copy(mask_in.at[:, lanes], MI.at[t], in_sem.at[5 * t + 4]),
        ]
    for load in loads:
        load.start()

    omegas = []
    for k in range(2):
        omega = jnp.float32(OMEGA_TABLE[k])
        for group in range(1, n_cons):
            omega = jnp.where(c == group, jnp.float32(OMEGA_TABLE[2 * group + k]), omega)
        omegas.append(omega)

    first_row = ty * rows_dev
    AX[...] = latitude_factor(
        first_row + lax.broadcasted_iota(jnp.int32, (rows_dev, LANES), 0), rows_dev * n_ty
    )
    ax_across = [
        latitude_factor(
            first_row + overlap * h + lax.broadcasted_iota(jnp.int32, (1, LANES), 1), rows_dev * n_ty
        )
        for h in range(2)
    ]

    lane = lax.broadcasted_iota(jnp.int32, (8, LANES), 1)
    lane_0, lane_last = lane == 0, lane == LANES - 1

    def arrive(tiles_now, copies):
        for load in copies:
            load.wait()

        @pl.loop(0, blocks, unroll=6)
        def _(b):
            for t in tiles_now:
                M[t, pl.ds(PAD + 8 * b, 8), :] = MI[t, pl.ds(8 * b, 8), :].astype(jnp.float32)

    arrive(outer_tiles, loads[:10])

    def plane_of(p, t, rows, eta, extras):
        if p < 4:
            return eta[p // 2, p % 2, t, rows, :] - Q[p // 2, p % 2, t, rows, :]
        return extras[p - 4][t, rows, :]

    def pack_columns(which, eta, extras):
        @pl.loop(0, blocks, unroll=6)
        def _(b):
            rows = pl.ds(PAD + 8 * b, 8)
            packed = jnp.zeros((8, LANES), jnp.float32)
            for p in range(4 + len(extras)):
                first = plane_of(p, 0, rows, eta, extras)
                last = plane_of(p, tiles - 1, rows, eta, extras)
                packed = jnp.where(lane == p, pltpu.roll(first, p, 1) if p else first, packed)
                packed = jnp.where(lane == 8 + p, pltpu.roll(last, 9 + p, 1), packed)
            PK[pl.ds(8 * b, 8), :] = packed

        for h in range(2):
            turned = PK[overlap * h : overlap * h + LANES, :].T
            col_out[which, 0, h] = turned[0:8]
            col_out[which, 1, h] = turned[8:16]

    def pack_rows(which, eta, extras):
        for t in range(tiles):
            for p in range(4 + len(extras)):
                row_out[which, 0, t, p : p + 1, :] = plane_of(p, t, pl.ds(PAD, 1), eta, extras)
                row_out[which, 1, t, p : p + 1, :] = plane_of(p, t, pl.ds(last_row - 1, 1), eta, extras)

    def halo_copies(which):
        copies = []
        for side, (source, target, there) in enumerate(
            (
                (col_out.at[which, 0], col_in.at[which, 1], {"tx": west}),
                (col_out.at[which, 1], col_in.at[which, 0], {"tx": east}),
                (row_out.at[which, 0], row_in.at[which, 1], {"ty": south}),
                (row_out.at[which, 1], row_in.at[which, 0], {"ty": north}),
            )
        ):
            copies.append(
                pltpu.make_async_remote_copy(
                    source, target, halo_send.at[4 * which + side], halo_recv.at[4 * which + side],
                    device_id=there, device_id_type=MESH,
                )
            )
        return copies

    groups = [(inner_tiles, a, (b - a) // 2, (b - a) // 2) for a, b in INNER] + [(inner_tiles, 0, 1, blocks - 1)]
    groups += [(outer_tiles, a, (b - a) // 2, (b - a) // 2) for a, b in OUTER]
    edges = len(INNER)

    def piece(g, owner):
        pair, first, count, step = groups[g]
        tile = pair[0] + (pair[1] - pair[0]) * (owner // 2)
        start = PAD + 8 * first + (8 * step) * lax.rem(owner, 2)
        return tile, pl.ds(pl.multiple_of(start, 8), 8 * count)

    def landing(g):
        start = 8 * sum(group[2] for group in groups[:g])
        return pl.ds(start, 8 * groups[g][2])

    def part_copy(g, d):
        tile, rows = piece(g, others[d - 1])
        return pltpu.make_async_remote_copy(
            S.at[tile, rows, :], part_in.at[d - 1, landing(g), :],
            part_send.at[g, d - 1], part_recv.at[g, d - 1],
            device_id={"cons": others[d - 1]}, device_id_type=MESH,
        )

    def rate_copy(g, d, source):
        tile, rows = piece(g, source)
        return pltpu.make_async_remote_copy(
            FR.at[tile, rows, :], FR.at[tile, rows, :],
            rate_send.at[g, d - 1], rate_recv.at[g, d - 1],
            device_id={"cons": others[d - 1]}, device_id_type=MESH,
        )

    def send_parts(g):
        for d in FAR_FIRST:
            part_copy(g, d).start()

    def settle(g):
        for d in FAR_FIRST:
            part_copy(g, d).wait_recv()
        tile, rows = piece(g, c)
        total = S[tile, rows, :]
        for d in FAR_FIRST:
            total = total + part_in[d - 1, landing(g), :]
        FR[tile, rows, :] = rate_of(total, D[tile, rows, :])
        for d in FAR_FIRST:
            rate_copy(g, d, c).start()

    def gathered(g):
        for d in FAR_FIRST:
            rate_copy(g, d, owners[d - 1]).wait_recv()

    def faces(mask, mask_next, deep, deep_next, scale):
        return -(mask * mask_next) * (0.5 * (deep + deep_next)) * scale

    def both_inverses(ru, rv, au, av, omega):
        square = omega * omega
        du, dv = ru * ru + square, rv * rv + square
        inverse = 1.0 / (du * dv)
        return au * (dv * inverse), av * (du * inverse)

    def northward(R, eta, fresh, start, which_tiles):
        rows, rows_n = pl.ds(start, 8), pl.ds(start + 1, 8)
        for t in which_tiles:
            if fresh:
                av = faces(M[t, rows, :], M[t, rows_n, :], D[t, rows, :], D[t, rows_n, :], AY_SCALE)
                AV[t, rows, :] = av
            else:
                av = AV[t, rows, :]
            rv = 0.5 * (R[t, rows, :] + R[t, rows_n, :])
            for k in range(2):
                over = av / (rv * rv + omegas[k] * omegas[k])
                d = [
                    (eta[k, p, t, rows_n, :] - Q[k, p, t, rows_n, :]) - (eta[k, p, t, rows, :] - Q[k, p, t, rows, :])
                    for p in range(2)
                ]
                v = face_flow(d[0], d[1], rv, over, omegas[k])
                for p in range(2):
                    V[k, p, t, rows, :] = v[p]

    def half_sweep(b, R, eta, fresh, inner):
        rows, rows_n, rows_s = pl.ds(PAD + 8 * b, 8), pl.ds(PAD + 8 * b + 1, 8), pl.ds(PAD + 8 * b - 1, 8)
        ax = AX[pl.ds(8 * b, 8), :]
        flowing = tuple(range(tiles - 1)) if inner else (tiles - 1,)
        closing = inner_tiles if inner else outer_tiles
        rim = None if inner else PH[pl.ds(8 * b, 8), :]

        def views(load, p):
            values = {t: load(t) for t in flowing}
            rolled = {t: pltpu.roll(values[t], LANES - 1, 1) for t in flowing}
            if inner:
                rolled[tiles - 1] = pltpu.roll(load(tiles - 1), LANES - 1, 1)
            else:
                rolled[tiles] = pltpu.roll(rim, (2 * LANES - 1 - (8 + p)) % LANES, 1)
            return values, {t: jnp.where(lane_last, rolled[t + 1], rolled[t]) for t in flowing}

        rate, rate_east = views(lambda t: R[t, rows, :], 4)
        if fresh:
            deep, deep_east = views(lambda t: D[t, rows, :], 5)
            mask, mask_east = views(lambda t: M[t, rows, :], 6)
        au, av, ru, rv = {}, {}, {}, {}
        for t in flowing:
            if fresh:
                au[t] = faces(mask[t], mask_east[t], deep[t], deep_east[t], ax)
                av[t] = faces(mask[t], M[t, rows_n, :], deep[t], D[t, rows_n, :], AY_SCALE)
                AU[t, rows, :] = au[t]
                AV[t, rows, :] = av[t]
            else:
                au[t] = AU[t, rows, :]
                av[t] = AV[t, rows, :]
            ru[t] = 0.5 * (rate[t] + rate_east[t])
            rv[t] = 0.5 * (rate[t] + R[t, rows_n, :])
        squares = {t: None for t in closing}
        theta_ax = THETA * ax
        for k in range(2):
            omega = omegas[k]
            theta_omega = THETA * omega
            zeta, zeta_east = [None, None], [None, None]
            for p in range(2):
                zeta[p], zeta_east[p] = views(lambda t: eta[k, p, t, rows, :] - Q[k, p, t, rows, :], 2 * k + p)
            flow_u, flow_v = [{}, {}], [{}, {}]
            for t in flowing:
                over_u, over_v = both_inverses(ru[t], rv[t], au[t], av[t], omega)
                u = face_flow(
                    zeta_east[0][t] - zeta[0][t], zeta_east[1][t] - zeta[1][t], ru[t], over_u, omega
                )
                north_z = [eta[k, p, t, rows_n, :] - Q[k, p, t, rows_n, :] for p in range(2)]
                v = face_flow(north_z[0] - zeta[0][t], north_z[1] - zeta[1][t], rv[t], over_v, omega)
                for p in range(2):
                    flow_u[p][t], flow_v[p][t] = u[p], v[p]
                    V[k, p, t, rows, :] = v[p]
            west_u = [{}, {}]
            for p in range(2):
                if inner:
                    rolled = {t: pltpu.roll(flow_u[p][t], 1, 1) for t in flowing}
                    U0[k, p, pl.ds(8 * b, 8), :] = flow_u[p][0]
                    U2[k, p, pl.ds(8 * b, 8), :] = rolled[tiles - 2]
                else:
                    q = 2 * k + p
                    flow_u[p][0] = U0[k, p, pl.ds(8 * b, 8), :]
                    flow_v[p][0] = V[k, p, 0, rows, :]
                    rolled = {t: pltpu.roll(flow_u[p][t], 1, 1) for t in closing}
                    rolled[-1] = pltpu.roll(rim, LANES - q, 1) if q else rim
                    rolled[tiles - 2] = U2[k, p, pl.ds(8 * b, 8), :]
                for t in closing:
                    west_u[p][t] = jnp.where(lane_0, rolled[t - 1], rolled[t])
            for t in closing:
                old = [eta[k, p, t, rows, :] for p in range(2)]
                wet = M[t, rows, :]
                for p in range(2):
                    south_v = V[k, p, t, rows_s, :]
                    turned = old[p] + theta_omega * old[1] if p == 0 else old[p] - theta_omega * old[0]
                    new = wet * (
                        turned
                        - theta_ax * (flow_u[p][t] - west_u[p][t])
                        - (THETA * AY_SCALE) * (flow_v[p][t] - south_v)
                    )
                    if fresh:
                        E1[k, p, t, rows, :] = new
                        cu = flow_u[p][t] + west_u[p][t]
                        cv = flow_v[p][t] + south_v
                        term = cu * cu + cv * cv
                        squares[t] = term if squares[t] is None else squares[t] + term
                    else:
                        out_e[k, p, pl.ds(8 * b, 8), LANES * t : LANES * (t + 1)] = new
        for t in closing:
            if fresh:
                S[t, rows, :] = squares[t]
            else:
                out_f[pl.ds(8 * b, 8), LANES * t : LANES * (t + 1)] = R[t, rows, :]

    def run(span, R, eta, fresh, inner):
        @pl.loop(span[0], span[1], unroll=unroll_of(span[1] - span[0]))
        def _(b):
            half_sweep(b, R, eta, fresh, inner)

    pack_columns(0, E, (F, D, M))
    arrive(inner_tiles, loads[10:])
    pack_rows(0, E, (F, D, M))
    pl.semaphore_wait(barrier, len(met))
    halo_one = halo_copies(0)
    for copy in halo_one:
        copy.start()
    northward(F, E, True, PAD, inner_tiles)
    for g in (0, 1):
        run(INNER[g], F, E, True, True)
        send_parts(g)
    for copy in halo_one[:2]:
        copy.wait_recv()

    def western_flow(h, which, rate):
        own, other = col_out.at[which, 0, h], col_in.at[which, 0, h]
        here, there = col_out.at[0, 0, h], col_in.at[0, 0, h]
        scale = faces(here[6:7, :], there[6:7, :], here[5:6, :], there[5:6, :], ax_across[h])
        for k in range(2):
            over = scale / (rate * rate + omegas[k] * omegas[k])
            d_re = own[2 * k : 2 * k + 1, :] - other[2 * k : 2 * k + 1, :]
            d_im = own[2 * k + 1 : 2 * k + 2, :] - other[2 * k + 1 : 2 * k + 2, :]
            u_re, u_im = face_flow(d_re, d_im, rate, over, omegas[k])
            HT[h, 2 * k : 2 * k + 1, :] = u_re
            HT[h, 2 * k + 1 : 2 * k + 2, :] = u_im

    def turn_back():
        PH[0:LANES, :] = HT[0].T
        PH[LANES:rows_dev, :] = HT[1].T[LANES - overlap :]

    for h in range(2):
        HT[h] = jnp.zeros((LANES, LANES), jnp.float32)
        HT[h, 8:16, :] = col_in[0, 1, h]
        western_flow(h, 0, 0.5 * (col_out[0, 0, h, 4:5, :] + col_in[0, 0, h, 4:5, :]))
    turn_back()
    for copy in halo_one[2:]:
        copy.wait_recv()

    inside_north = jnp.where(ty == n_ty - 1, jnp.float32(0), jnp.float32(1))
    inside_south = jnp.where(ty == 0, jnp.float32(0), jnp.float32(1))
    for t in range(tiles):
        for side, row, keep in ((0, PAD - 1, inside_south), (1, last_row, inside_north)):
            line = pl.ds(row, 1)
            for p in range(4):
                E[p // 2, p % 2, t, line, :] = row_in[0, side, t, p : p + 1, :]
                Q[p // 2, p % 2, t, line, :] = jnp.zeros((1, LANES), jnp.float32)
            F[t, line, :] = row_in[0, side, t, 4:5, :]
            D[t, line, :] = row_in[0, side, t, 5:6, :]
            M[t, line, :] = row_in[0, side, t, 6:7, :] * keep
    northward(F, E, True, 0, range(tiles))
    for b in (0, blocks - 1):
        half_sweep(b, F, E, True, True)
    send_parts(edges)
    first_outer = edges + 1
    for i, span in enumerate(OUTER):
        run(span, F, E, True, False)
        send_parts(first_outer + i)

    halo_two = halo_copies(1)
    pack_rows(1, E1, (S,))
    for copy in halo_two[2:]:
        copy.start()
    pack_columns(1, E1, (S,))
    for copy in halo_two[:2]:
        copy.start()
    for g in range(first_outer):
        settle(g)
    settle(first_outer)
    for copy in halo_two:
        copy.wait_recv()
    for t in range(tiles):
        ring_out[t : t + 1, :] = row_in[1, 0, t, 4:5, :]
        ring_out[tiles + t : tiles + t + 1, :] = row_in[1, 1, t, 4:5, :]
    for h in range(2):
        ring_out[8 + h : 9 + h, :] = col_in[1, 0, h, 4:5, :]
        ring_out[10 + h : 11 + h, :] = col_in[1, 1, h, 4:5, :]
        ring_out[12 + h : 13 + h, :] = col_out[1, 0, h, 4:5, :]
    ring_out[14:16, :] = jnp.zeros((2, LANES), jnp.float32)
    ring = [
        pltpu.make_async_remote_copy(
            ring_out, ring_in.at[d - 1], ring_send.at[d - 1], ring_recv.at[d - 1],
            device_id={"cons": others[d - 1]}, device_id_type=MESH,
        )
        for d in range(1, n_cons)
    ]
    for copy in ring:
        copy.start()
    for g in range(first_outer + 1, len(groups)):
        settle(g)

    for g in (0, edges, first_outer):
        gathered(g)
    northward(FR, E1, False, PAD, inner_tiles)
    gathered(1)
    run((1, 11), FR, E1, False, True)

    for copy in ring:
        copy.wait_recv()

    def ring_rate(line, depth):
        rows = slice(line, line + 1)
        total = (ring_out[rows, :] + ring_in[0, rows, :]) + (ring_in[1, rows, :] + ring_in[2, rows, :])
        return rate_of(total, depth)

    for t in range(tiles):
        for side, row in ((0, PAD - 1), (1, last_row)):
            line = pl.ds(row, 1)
            for p in range(4):
                E1[p // 2, p % 2, t, line, :] = row_in[1, side, t, p : p + 1, :]
            FR[t, line, :] = ring_rate(tiles * side + t, row_in[0, side, t, 5:6, :])
    for h in range(2):
        rate_west = ring_rate(8 + h, col_in[0, 0, h, 5:6, :])
        rate_east = ring_rate(10 + h, col_in[0, 1, h, 5:6, :])
        rate_own = ring_rate(12 + h, col_out[0, 0, h, 5:6, :])
        HT[h, 8:12, :] = col_in[1, 1, h, 0:4, :]
        HT[h, 12:13, :] = rate_east
        western_flow(h, 1, 0.5 * (rate_own + rate_west))
    turn_back()
    northward(FR, E1, False, 0, range(tiles))
    half_sweep(0, FR, E1, False, True)
    run((0, 3), FR, E1, False, False)
    run((3, 11), FR, E1, False, False)
    gathered(first_outer + 1)
    run((11, 17), FR, E1, False, True)
    half_sweep(blocks - 1, FR, E1, False, True)
    run((11, 15), FR, E1, False, False)
    run((15, blocks), FR, E1, False, False)

    for copy in halo_one + halo_two + ring:
        copy.wait_send()
    for g in range(len(groups)):
        for d in FAR_FIRST:
            part_copy(g, d).wait_send()
            rate_copy(g, d, c).wait_send()


def put_out(e_ref, f_ref, e_out, f_out, sem):
    copies = [
        pltpu.make_async_copy(e_ref.at[k, p], e_out.at[k, p], sem.at[2 * k + p]) for k in range(2) for p in range(2)
    ]
    copies.append(pltpu.make_async_copy(f_ref, f_out, sem.at[4]))
    for copy in copies:
        copy.start()
    for copy in copies:
        copy.wait()


def solution(mesh):
    n_cons, n_ty, n_tx = (mesh.shape[axis] for axis in ("cons", "ty", "tx"))

    def body(elevation, equilibrium, depth, land_mask, friction_prev):
        kdev, two, rows_dev, cols_dev = elevation.shape
        tiles = cols_dev // LANES
        tall = rows_dev + 2 * PAD
        f32 = jnp.float32
        field = pltpu.VMEM((tiles, tall, LANES), f32)
        fields = pltpu.VMEM((2, 2, tiles, tall, LANES), f32)
        n_groups = len(INNER) + len(OUTER) + 1
        hbm = pl.BlockSpec(memory_space=pltpu.HBM)
        vmem = pl.BlockSpec(memory_space=pltpu.VMEM)
        moved = pl.pallas_call(
            functools.partial(kernel, (rows_dev, tiles, n_cons, n_ty, n_tx)),
            out_shape=(
                pltpu.VMEM(elevation.shape, f32),
                pltpu.VMEM(depth.shape, f32),
            ),
            in_specs=[hbm] * 5,
            out_specs=(vmem, vmem),
            scratch_shapes=[
                fields, fields, fields, field, field,
                pltpu.VMEM((tiles, rows_dev, LANES), jnp.int32),
                field, field, field,
                pltpu.VMEM((2, 2, rows_dev, LANES), f32),
                pltpu.VMEM((2, 2, rows_dev, LANES), f32),
                fields, field, field,
                pltpu.VMEM((rows_dev, LANES), f32),
                pltpu.VMEM((rows_dev, LANES), f32),
                pltpu.VMEM((2, LANES, LANES), f32),
                pltpu.VMEM((rows_dev, LANES), f32),
                pltpu.VMEM((2, 2, tiles, 8, LANES), f32),
                pltpu.VMEM((2, 2, tiles, 8, LANES), f32),
                pltpu.VMEM((2, 2, 2, 8, LANES), f32),
                pltpu.VMEM((2, 2, 2, 8, LANES), f32),
                pltpu.VMEM((16, LANES), f32),
                pltpu.VMEM((n_cons - 1, 16, LANES), f32),
                pltpu.VMEM((n_cons - 1, rows_dev, LANES), f32),
                pltpu.SemaphoreType.DMA((5 * tiles,)),
                pltpu.SemaphoreType.DMA((8,)),
                pltpu.SemaphoreType.DMA((8,)),
                pltpu.SemaphoreType.DMA((n_cons - 1,)),
                pltpu.SemaphoreType.DMA((n_cons - 1,)),
                pltpu.SemaphoreType.DMA((n_groups, n_cons - 1)),
                pltpu.SemaphoreType.DMA((n_groups, n_cons - 1)),
                pltpu.SemaphoreType.DMA((n_groups, n_cons - 1)),
                pltpu.SemaphoreType.DMA((n_groups, n_cons - 1)),
            ],
            compiler_params=pltpu.CompilerParams(collective_id=0, has_side_effects=True, vmem_limit_bytes=56 * 2**20),
        )(elevation, equilibrium, depth, land_mask, friction_prev)
        return pl.pallas_call(
            put_out,
            out_shape=(
                jax.ShapeDtypeStruct(elevation.shape, f32),
                jax.ShapeDtypeStruct(depth.shape, f32),
            ),
            in_specs=[pl.BlockSpec(memory_space=pl.ANY)] * 2,
            out_specs=(hbm, hbm),
            scratch_shapes=[pltpu.SemaphoreType.DMA((5,))],
            compiler_params=pltpu.CompilerParams(vmem_limit_bytes=8 * 2**20),
        )(*moved)

    tiled = P("ty", "tx")
    planes = P("cons", None, "ty", "tx")
    return jax.shard_map(
        body,
        mesh=mesh,
        in_specs=(planes, planes, tiled, tiled, tiled),
        out_specs=(planes, tiled),
        check_vma=False,
    )
```
